32 devices in a mesh: seq: 8 (over y, x, core), req: 4 (over z).
Axes of the slice: x: 2, y: 2, z: 4, core: 2. Of those that a mesh axis runs over, the one named last changes fastest.
Arguments:
- queries: bfloat16 [8, 256, 1536], P('req', 'seq'), as said below
- new_kv: bfloat16 [2, 8, 256, 512], P(None, 'req', 'seq'), may hold values from -6 to 6
- cache_kv: bfloat16 [2, 8, 2048, 512], P(None, 'req', 'seq'), as said below
- cache_spans: int32 [8, 2], P('req'), may hold values from 0 to 2048, as said below
- recompute_rows: int32 [8, 256], P('req'), may hold values from 0 to 2047, as said below
- held_states: bfloat16 [8, 256, 1536], P('req', 'seq'), may hold values from -6 to 6
- key_weight: bfloat16 [1536, 512], replicated, may hold values from -0.15625 to 0.15625
- norm_gain: float32 [1536], replicated, may hold values from 0.1 to 1.9
- routes: int32 [8, 256, 8], P('req', 'seq'), may hold values from 0 to 19, all different within a row; in each aligned block of 32 rows (0 to 31, 32 to 63, ..., all dimensions but the last counted through in order) at most 16 rows name the same one
- route_weights: float32 [8, 256, 8], P('req', 'seq'), may hold values from 0.05 to 1
- expert_gate_up: bfloat16 [20, 1536, 1024], P('req'), may hold values from -0.15625 to 0.15625
- expert_down: bfloat16 [20, 512, 1536], P('req'), may hold values from -0.25 to 0.25
Outputs:
- layer_out: bfloat16 [8, 256, 1536], P('req', 'seq')
The draws below stay inside these ranges and needn't reach their ends.
Inputs may be any that keep to these rules, and one draw needn't show every extreme that they name: `routes`: in each aligned block of 32 rows of one request (one device's rows of that request) no expert is named more than 16 times. cache_spans[r] = (start, length): 1024 <= length <= 2048 with some request of length 2048; 0 <= start <= 512 with some request starting at 0. `recompute_rows`: within a request the rows are distinct and lie between the request's start and length. `queries`: entries lie within -6 to 6. `cache_kv`: entries lie within -6 to 6.
All inputs are finite; a program needn't handle non-finite values.
Results may differ from the reference program's by a relative error of at most 0.034.
Values may be sent and summed in bfloat16 or wider, within the bound.
A program may use at most 192 MiB of HBM per device.

```python
import math
import jax
import jax.numpy as jnp
import numpy as np
from jax import lax

D = 1536
H = 24
KVH = 8
HD = 64
FF = 512
TOP = 8
STEP_DEV = 32
CAP = 16
EXPERTS = 20
REQUESTS = 8
STEP = 256
CACHE = 2048
RECOMP = 256


def draw_queries(key, part):
    values = jnp.clip(jax.random.normal(jax.random.fold_in(key, 1), (REQUESTS, STEP, H * HD), jnp.float32), -4.0, 4.0)
    return values.astype(jnp.bfloat16)


def draw_cache_kv(key, part):
    values = jnp.clip(jax.random.normal(jax.random.fold_in(key, 2), (2, REQUESTS, CACHE, KVH * HD), jnp.float32), -4.0, 4.0)
    return values.astype(jnp.bfloat16)


def span_table(key):
    folded = jax.random.fold_in(key, 5)
    key_length, key_pick, key_start, key_zero = jax.random.split(folded, 4)
    lengths = jax.random.randint(key_length, (REQUESTS,), CACHE // 2, CACHE + 1)
    lengths = jnp.where(jnp.arange(REQUESTS) == jax.random.randint(key_pick, (), 0, REQUESTS), CACHE, lengths)
    starts = jax.random.randint(key_start, (REQUESTS,), 0, CACHE // 4 + 1)
    starts = jnp.where(jnp.arange(REQUESTS) == jax.random.randint(key_zero, (), 0, REQUESTS), 0, starts)
    return (starts, lengths)


def draw_cache_spans(key, part):
    starts, lengths = span_table(key)
    return jnp.stack([starts, lengths], axis=1).astype(jnp.int32)


def draw_recompute_rows(key, part):
    starts, lengths = span_table(key)
    stride = (lengths - starts) // RECOMP
    offsets = jax.random.randint(jax.random.fold_in(key, 9), (REQUESTS, RECOMP), 0, 1 << 20) % stride[:, None]
    rows = starts[:, None] + jnp.arange(RECOMP)[None, :] * stride[:, None] + offsets
    column = jnp.arange(RECOMP)[None, :]
    rows = jnp.where(column == 0, starts[:, None], rows)
    rows = jnp.where(column == RECOMP - 1, lengths[:, None] - 1, rows)
    return rows.astype(jnp.int32)


def block_scale(key, dims, shards, low, high):
    factor_of = 1.0
    for dim, blocks in shards:
        steps = jax.random.uniform(jax.random.fold_in(jax.random.fold_in(key, 6), dim), (blocks,), jnp.float32, low / len(shards), high / len(shards))
        factor_of = factor_of * jnp.repeat(jnp.exp(steps), dims[dim] // blocks).reshape((-1,) + (1,) * (len(dims) - 1 - dim))
    return factor_of


def routed_block(stream_key, own, number, rows, amount, top, bound, skew):
    order = jax.random.permutation(stream_key, amount)
    crowded, usual = shares(amount, rows * top, bound, skew, True), shares(amount, rows * top, bound, skew, False)
    places = jnp.arange(amount)

    def named(tallies, rotation):
        used = int((tallies > 0).sum())
        fixed = max(1, used // 4)
        shifted = fixed + (places - fixed + rotation * (used - fixed)) % max(1, amount - fixed)
        return jnp.zeros((amount,), jnp.int32).at[order[jnp.where(places < fixed, places, shifted)]].set(jnp.asarray(tallies, jnp.int32))

    tallies = jnp.where(number % 4 == 0, named(crowded, number // 4), named(usual, number - number // 4 - 1))
    mixed = jax.random.permutation(jax.random.fold_in(own, 3), amount)
    giver, sink = mixed[0:amount // 2 * 2:2], mixed[1:amount // 2 * 2:2]
    room = jnp.minimum(tallies[giver] - 1, bound - tallies[sink]) // 2
    room = jnp.where((giver == order[0]) | (sink == order[0]) | (tallies[sink] == 0), 0, jnp.maximum(room, 0))
    shifted = jax.random.randint(jax.random.fold_in(own, 4), (amount // 2,), 0, 1 << 20) % (room + 1)
    tallies = tallies.at[giver].add(-shifted).at[sink].add(shifted)
    members = jnp.searchsorted(jnp.cumsum(tallies), jnp.arange(rows * top), side="right").astype(jnp.int32)
    grid = members.reshape(top, rows).T
    grid = grid[jax.random.permutation(jax.random.fold_in(own, 1), rows)]
    rotation = jax.random.randint(jax.random.fold_in(own, 2), (rows, 1), 0, top)
    return jnp.take_along_axis(grid, (jnp.arange(top)[None, :] + rotation) % top, axis=1)


def shares(count, total, reach, skew, full):
    loads = [(1 << 20) // math.isqrt(standing ** skew) + 1 for standing in range(1, count + 1)]
    largest = reach if full else min(reach, max(-(-total // count), total * loads[0] // sum(loads)))
    least = 1 if total - largest >= count - 1 else 0
    holding, surplus = [largest] + [least] * (count - 1), total - largest - least * (count - 1)
    while surplus > 0:
        candidates = [i for i in range(1, count) if holding[i] < largest] or [i for i in range(1, count) if holding[i] < reach]
        pool, budget = sum([loads[i] for i in candidates]), surplus
        for i in candidates:
            addition = min(reach - holding[i], max(1, budget * loads[i] // pool), surplus)
            holding[i] = holding[i] + addition
            surplus = surplus - addition
    return np.array(holding)


def noise(key, extent, scale, limit, cuts=(), kind=jnp.bfloat16):
    array = jax.random.normal(key, extent, jnp.float32) * scale
    if len(cuts) > 0:
        array = block_scale(key, extent, cuts, -0.22, 0.18) * array
    return jnp.clip(array, min=-limit, max=limit).astype(kind)


def setup_inputs(seed: int = 0) -> dict:
    streams_of = jax.random.split(jax.random.key(seed), 13)
    queries = draw_queries(jax.random.fold_in(streams_of[12], 71), 0)
    new_kv = noise(streams_of[1], (2, REQUESTS, STEP, KVH * HD), 1.0, 6.0, ((1, 4), (2, 8)))
    cache_kv = draw_cache_kv(jax.random.fold_in(streams_of[12], 71), 0)
    cache_spans = draw_cache_spans(jax.random.fold_in(streams_of[12], 71), 0)
    recompute_rows = draw_recompute_rows(jax.random.fold_in(streams_of[12], 71), 0)
    held_states = noise(streams_of[5], (REQUESTS, RECOMP, D), 1.0, 6.0, ((0, 4), (1, 8)))
    key_weight = noise(streams_of[6], (D, KVH * HD), D ** -0.5, 0.15625)
    norm_gain = jnp.clip(1.0 + 0.18 * jax.random.normal(streams_of[7], (D,), jnp.float32), 0.1, 1.9)
    routes_keys = jax.random.split(jax.random.fold_in(streams_of[8], 1), REQUESTS * STEP // STEP_DEV)
    routes_turns = jax.random.permutation(jax.random.fold_in(streams_of[8], 3), REQUESTS * STEP // STEP_DEV)
    routes = jax.vmap(lambda own, number: routed_block(jax.random.fold_in(streams_of[8], 2), own, number, STEP_DEV, EXPERTS, TOP, CAP, 1))(routes_keys, routes_turns).reshape((REQUESTS, STEP, TOP))
    route_weights = jnp.clip(0.05 + 0.95 * jax.random.uniform(streams_of[9], (REQUESTS, STEP, TOP), jnp.float32) ** block_scale(streams_of[9], (REQUESTS, STEP, TOP), ((0, 4), (1, 8)), -0.2, 0.2), 0.05, 1.0)
    expert_gate_up = noise(streams_of[10], (EXPERTS, D, 2 * FF), D ** -0.5, 0.15625, ((0, 4),))
    expert_down = noise(streams_of[11], (EXPERTS, FF, D), FF ** -0.5, 0.25, ((0, 4),))
    return {"queries": queries, "new_kv": new_kv, "cache_kv": cache_kv, "cache_spans": cache_spans, "recompute_rows": recompute_rows, "held_states": held_states, "key_weight": key_weight, "norm_gain": norm_gain, "routes": routes, "route_weights": route_weights, "expert_gate_up": expert_gate_up, "expert_down": expert_down}


NEG = -1e+30
THETA = 10000.0

def rotate(key_heads, positions):
    half_dim = key_heads.shape[-1] // 2
    exponent = jnp.arange(half_dim).astype(jnp.float32) * (2.0 / key_heads.shape[-1])
    inverse = THETA ** (-exponent)
    angles = positions.astype(jnp.float32)[..., None] * inverse
    cosine = jnp.cos(angles)[..., None, :]
    sine_part = jnp.sin(angles)[..., None, :]
    lower_half = key_heads[..., :half_dim]
    upper_half = key_heads[..., half_dim:]
    return jnp.concatenate([lower_half * cosine - upper_half * sine_part, upper_half * cosine + lower_half * sine_part], axis=-1)

def attend_request(packed):
    query_rows, cache_key_rows, cache_value_rows, step_key_rows, step_value_rows, span_pair = packed
    groups = H // KVH
    key_heads = jnp.concatenate([cache_key_rows, step_key_rows], axis=0).astype(jnp.float32).reshape(CACHE + STEP, KVH, HD)
    value_heads = jnp.concatenate([cache_value_rows, step_value_rows], axis=0).astype(jnp.float32).reshape(CACHE + STEP, KVH, HD)
    query_heads = query_rows.astype(jnp.float32).reshape(STEP, KVH, groups, HD)
    scores = jnp.einsum('qkgd,nkd->kgqn', query_heads, key_heads, precision=lax.Precision.HIGHEST) * HD ** (-0.5)
    cache_index = jnp.arange(CACHE).astype(jnp.int32)
    cache_allowed = (cache_index >= span_pair[0]) & (cache_index < span_pair[1])
    step_index = jnp.arange(STEP).astype(jnp.int32)
    step_allowed = step_index[None, :] <= step_index[:, None]
    allowed = jnp.concatenate([jnp.broadcast_to(cache_allowed[None, :], (STEP, CACHE)), step_allowed], axis=1)
    scores = jnp.where(allowed[None, None], scores, NEG)
    highest = lax.optimization_barrier(jnp.max(scores, axis=-1, keepdims=True))
    exps = jnp.exp(scores - highest)
    totals = lax.optimization_barrier(jnp.sum(exps, axis=-1))
    weights = lax.optimization_barrier(exps.astype(jnp.bfloat16)).astype(jnp.float32)
    mixed_rows = jnp.einsum('kgqn,nkd->qkgd', weights, value_heads, precision=lax.Precision.HIGHEST)
    mixed_rows = mixed_rows / jnp.transpose(totals, (2, 0, 1))[..., None]
    return mixed_rows.reshape(STEP, D).astype(jnp.bfloat16)

def expert_outputs(normed, routes, expert_gate_up, expert_down):
    tile_rows = 256
    token_total = normed.shape[0] * normed.shape[1]
    flat_tokens = jnp.concatenate([normed.reshape(token_total, D), jnp.zeros((1, D), normed.dtype)], axis=0)
    flat_routes = routes.reshape(-1).astype(jnp.int32)
    route_total = flat_routes.shape[0]
    owner_token = (jnp.arange(route_total) // TOP).astype(jnp.int32)
    counts = lax.optimization_barrier(jnp.sum((flat_routes[:, None] == jnp.arange(EXPERTS).astype(jnp.int32)[None, :]).astype(jnp.int32), axis=0)).astype(jnp.int32)
    padded = ((counts + tile_rows - 1) // tile_rows * tile_rows).astype(jnp.int32)
    padded_start = (jnp.cumsum(padded) - padded).astype(jnp.int32)
    first_sorted = (jnp.cumsum(counts) - counts).astype(jnp.int32)
    sort_order = jnp.argsort(flat_routes, stable=True).astype(jnp.int32)
    sorted_experts = flat_routes[sort_order]
    rank_within = (jnp.arange(route_total).astype(jnp.int32) - first_sorted[sorted_experts]).astype(jnp.int32)
    destination = (padded_start[sorted_experts] + rank_within).astype(jnp.int32)
    block_count = (route_total + tile_rows - 1) // tile_rows + EXPERTS
    slot_token = jnp.full((block_count * tile_rows,), token_total, jnp.int32).at[destination].set(owner_token[sort_order])
    block_starts = (jnp.arange(block_count) * tile_rows).astype(jnp.int32)
    block_expert = (lax.optimization_barrier(jnp.sum((padded_start[None, :] <= block_starts[:, None]).astype(jnp.int32), axis=1)) - 1).astype(jnp.int32)

    def one_block(packed):
        token_ids, expert_id = packed
        row_block = flat_tokens[token_ids]
        hidden = jnp.dot(row_block, expert_gate_up[expert_id], preferred_element_type=jnp.float32)
        active = (jax.nn.silu(hidden[:, :FF]) * hidden[:, FF:]).astype(jnp.bfloat16)
        return jnp.dot(active, expert_down[expert_id], preferred_element_type=jnp.float32).astype(jnp.bfloat16)
    outputs = lax.map(one_block, (slot_token.reshape(block_count, tile_rows), block_expert))
    outputs = outputs.reshape(block_count * tile_rows, D)
    position = jnp.zeros((route_total,), jnp.int32).at[sort_order].set(destination)
    return outputs[position].reshape(normed.shape[0], normed.shape[1], TOP, D)

def reference(queries, new_kv, cache_kv, cache_spans, recompute_rows, held_states, key_weight, norm_gain, routes, route_weights, expert_gate_up, expert_down):
    projected = jnp.dot(held_states.reshape(REQUESTS * RECOMP, D), key_weight, preferred_element_type=jnp.float32)
    rotated = rotate(projected.reshape(REQUESTS, RECOMP, KVH, HD), recompute_rows)
    fresh_rows = rotated.reshape(REQUESTS, RECOMP, KVH * HD).astype(jnp.bfloat16)
    request_ids = jnp.arange(REQUESTS).astype(jnp.int32)[:, None]
    cache_keys = cache_kv[0].at[request_ids, recompute_rows.astype(jnp.int32)].set(fresh_rows)
    attended = lax.map(attend_request, (queries, cache_keys, cache_kv[1], new_kv[0], new_kv[1], cache_spans))
    attended_f = attended.astype(jnp.float32)
    mean_square = lax.optimization_barrier(jnp.mean(attended_f * attended_f, axis=-1, keepdims=True))
    normed = (attended_f * lax.rsqrt(mean_square + 1e-06) * norm_gain).astype(jnp.bfloat16)
    routed = expert_outputs(normed, routes, expert_gate_up, expert_down)
    mixture = jnp.einsum('rtk,rtkd->rtd', route_weights, routed.astype(jnp.float32), precision=lax.Precision.HIGHEST)
    return (attended_f + mixture).astype(jnp.bfloat16)
```

```python
import jax
import jax.numpy as jnp
from jax import lax
from jax.sharding import PartitionSpec as P

H = 24
KVH = 8
HD = 64
FF = 512
TOP = 8
CAP = 16


NEG = -1e30
THETA = 10000.0


def rotate(key_heads, positions):
    half_dim = key_heads.shape[-1] // 2
    exponent = jnp.arange(half_dim).astype(jnp.float32) * (2.0 / key_heads.shape[-1])
    inverse = THETA ** (-exponent)
    angles = positions.astype(jnp.float32)[..., None] * inverse
    cosine = jnp.cos(angles)[..., None, :]
    sine_part = jnp.sin(angles)[..., None, :]
    lower_half = key_heads[..., :half_dim]
    upper_half = key_heads[..., half_dim:]
    return jnp.concatenate(
        [
            lower_half * cosine - upper_half * sine_part,
            upper_half * cosine + lower_half * sine_part,
        ],
        axis=-1,
    )


def partial_attend(packed):
    query_rows, key_rows, value_rows, allowed = packed
    query_count, model_width = query_rows.shape
    key_count = key_rows.shape[0]
    groups = H // KVH
    query_heads = query_rows.reshape(query_count, KVH, groups, HD)
    key_heads = key_rows.reshape(key_count, KVH, HD)
    value_heads = value_rows.reshape(key_count, KVH, HD)
    scores = jnp.einsum(
        "qkgd,nkd->kgqn", query_heads, key_heads, preferred_element_type=jnp.float32
    ) * HD ** (-0.5)
    scores = jnp.where(allowed[None, None, :, :], scores, NEG)
    highest = jnp.max(scores, axis=-1, keepdims=True)
    exps = jnp.exp(scores - highest)
    totals = jnp.sum(exps, axis=-1)
    weights = exps.astype(jnp.bfloat16)
    mixed_rows = jnp.einsum(
        "kgqn,nkd->qkgd", weights, value_heads, preferred_element_type=jnp.float32
    )
    mixed_rows = mixed_rows / jnp.transpose(totals, (2, 0, 1))[..., None]
    log_total = highest[..., 0] + jnp.log(totals)
    log_rows = jnp.transpose(log_total, (2, 0, 1)).reshape(query_count, H)
    return (mixed_rows.reshape(query_count, model_width), log_rows)


def body_wide(
    queries,
    new_kv,
    cache_kv,
    cache_spans,
    recompute_rows,
    held_states,
    key_weight,
    norm_gain,
    routes,
    route_weights,
    expert_gate_up,
    expert_down,
):
    seq_index = lax.axis_index("seq")
    seq_count = lax.axis_size("seq")
    owner_count = lax.axis_size("req")
    req_rows, tok_rows, model_width = queries.shape
    cache_rows = cache_kv.shape[2]
    held_rows = held_states.shape[1]
    local_experts = expert_gate_up.shape[0]
    expert_total = owner_count * local_experts
    my_positions = lax.dynamic_slice_in_dim(recompute_rows, seq_index * held_rows, held_rows, 1)
    projected = jnp.dot(
        held_states.reshape(req_rows * held_rows, model_width),
        key_weight,
        preferred_element_type=jnp.float32,
    )
    rotated = rotate(projected.reshape(req_rows, held_rows, KVH, HD), my_positions)
    rotated = rotated.reshape(req_rows, held_rows, KVH * HD).astype(jnp.bfloat16)
    fresh_rows = lax.all_gather(rotated, "seq", axis=1, tiled=True)
    cache_positions = seq_index * cache_rows + jnp.arange(cache_rows)
    hit_table = recompute_rows[:, None, :] == cache_positions[None, :, None]
    placed = jnp.einsum(
        "rcm,rmk->rck",
        hit_table.astype(jnp.bfloat16),
        fresh_rows,
        preferred_element_type=jnp.float32,
    ).astype(jnp.bfloat16)
    cache_keys = jnp.where(jnp.any(hit_table, axis=2)[:, :, None], placed, cache_kv[0])
    span_start = cache_spans[:, 0:1]
    span_end = cache_spans[:, 1:2]
    all_queries = lax.all_gather(queries, "seq", axis=1, tiled=True)
    step_total = all_queries.shape[1]
    cache_allowed = (cache_positions[None, :] >= span_start) & (cache_positions[None, :] < span_end)
    key_positions = seq_index * tok_rows + jnp.arange(tok_rows)
    step_allowed = key_positions[None, :] <= jnp.arange(step_total)[:, None]
    allowed = jnp.concatenate(
        [
            jnp.broadcast_to(cache_allowed[:, None, :], (req_rows, step_total, cache_rows)),
            jnp.broadcast_to(step_allowed[None], (req_rows, step_total, tok_rows)),
        ],
        axis=2,
    )
    key_rows = jnp.concatenate([cache_keys, new_kv[0]], axis=1)
    value_rows = jnp.concatenate([cache_kv[1], new_kv[1]], axis=1)
    part_out, part_log = lax.map(partial_attend, (all_queries, key_rows, value_rows, allowed))
    piece_out, piece_log = (
        lax.all_to_all(part_out[None], "seq", split_axis=2, concat_axis=0, tiled=True),
        lax.all_to_all(part_log[None], "seq", split_axis=2, concat_axis=0, tiled=True),
    )
    best_log = jnp.max(piece_log, axis=0)
    factors = jnp.exp(piece_log - best_log[None])
    factor_sum = jnp.sum(factors, axis=0)
    spread_out = piece_out.reshape(seq_count, req_rows, tok_rows, H, HD)
    combined = jnp.sum(spread_out * factors[..., None], axis=0) / factor_sum[..., None]
    attended_f = combined.reshape(req_rows, tok_rows, model_width)
    attended = attended_f.astype(jnp.bfloat16)
    attended_f = attended.astype(jnp.float32)
    mean_square = jnp.mean(attended_f * attended_f, axis=-1, keepdims=True)
    normed = (attended_f * lax.rsqrt(mean_square + 1e-06) * norm_gain).astype(jnp.bfloat16)
    route_flat = routes.reshape(req_rows, tok_rows * TOP)
    expert_match = (route_flat[:, :, None] == jnp.arange(expert_total)[None, None, :]).astype(
        jnp.int32
    )
    earlier = jnp.cumsum(expert_match, axis=1) - expert_match
    slot_index = jnp.sum(earlier * expert_match, axis=2)
    target = route_flat * CAP + slot_index
    slot_match = target[:, :, None] == jnp.arange(expert_total * CAP)[None, None, :]
    dispatch = jnp.any(
        slot_match.reshape(req_rows, tok_rows, TOP, expert_total * CAP), axis=2
    ).astype(jnp.bfloat16)
    dispatch = dispatch.reshape(req_rows, tok_rows, owner_count, local_experts, CAP)
    outgoing = jnp.einsum(
        "rtnec,rtd->nrecd", dispatch, normed, preferred_element_type=jnp.float32
    ).astype(jnp.bfloat16)
    hidden = jnp.einsum(
        "srecd,edf->srecf",
        lax.all_to_all(outgoing, "req", split_axis=0, concat_axis=0, tiled=True),
        expert_gate_up,
        preferred_element_type=jnp.float32,
    )
    active = (jax.nn.silu(hidden[..., :FF]) * hidden[..., FF:]).astype(jnp.bfloat16)
    result = jnp.einsum(
        "srecf,efd->srecd", active, expert_down, preferred_element_type=jnp.float32
    ).astype(jnp.bfloat16)
    returned = lax.all_to_all(result, "req", split_axis=0, concat_axis=0, tiled=True)
    owner_of = route_flat // local_experts
    local_of = route_flat % local_experts
    flat_index = (
        (owner_of * req_rows + jnp.arange(req_rows)[:, None]) * local_experts + local_of
    ) * CAP + slot_index
    returned_rows = jnp.take(returned.reshape(-1, model_width), flat_index.reshape(-1), axis=0)
    returned_rows = returned_rows.reshape(req_rows, tok_rows, TOP, model_width)
    mixture = jnp.einsum(
        "rtk,rtkd->rtd",
        route_weights,
        returned_rows.astype(jnp.float32),
        precision=lax.Precision.HIGHEST,
    )
    return (attended_f + mixture).astype(jnp.bfloat16)


def head_parallel_body(
    queries,
    new_kv,
    cache_kv,
    cache_spans,
    recompute_rows,
    held_states,
    key_weight,
    norm_gain,
    routes,
    route_weights,
    expert_gate_up,
    expert_down,
):
    seq_index = lax.axis_index("seq")
    seq_count = lax.axis_size("seq")
    req_index = lax.axis_index("req")
    owner_count = lax.axis_size("req")
    req_rows, tok_rows, model_width = queries.shape
    cache_rows = cache_kv.shape[2]
    held_rows = held_states.shape[1]
    local_experts = expert_gate_up.shape[0]
    groups = H // KVH
    bf16 = jnp.bfloat16
    f32 = jnp.float32
    my_positions = lax.dynamic_slice_in_dim(recompute_rows, seq_index * held_rows, held_rows, 1)
    projected = jnp.dot(
        held_states.reshape(req_rows * held_rows, model_width),
        key_weight,
        preferred_element_type=f32,
    )
    rotated = rotate(projected.reshape(req_rows, held_rows, KVH, HD), my_positions).astype(bf16)
    kv = jnp.concatenate([cache_kv, new_kv], axis=2)
    kv = kv.reshape(2, req_rows, cache_rows + tok_rows, KVH, HD).transpose(3, 1, 2, 0, 4)
    kv = kv.reshape(KVH, req_rows, cache_rows + tok_rows, 2 * HD)
    kv = lax.all_to_all(kv, "seq", split_axis=0, concat_axis=0, tiled=True)
    query_pack = queries.reshape(req_rows, tok_rows, KVH, groups * HD).transpose(2, 0, 1, 3)
    query_pack = lax.all_to_all(query_pack, "seq", split_axis=0, concat_axis=0, tiled=True)
    fresh = lax.all_to_all(
        rotated.transpose(2, 0, 1, 3), "seq", split_axis=0, concat_axis=0, tiled=True
    )
    fresh = fresh.transpose(1, 0, 2, 3).reshape(req_rows, seq_count * held_rows, HD)
    cache_total = seq_count * cache_rows
    step_total = seq_count * tok_rows
    cache_part = kv[:, :, :cache_rows].transpose(1, 0, 2, 3).reshape(req_rows, cache_total, 2 * HD)
    step_part = kv[:, :, cache_rows:].transpose(1, 0, 2, 3).reshape(req_rows, step_total, 2 * HD)
    positions = jnp.arange(cache_total)
    hit_table = recompute_rows[:, None, :] == positions[None, :, None]
    placed = jnp.einsum(
        "rcm,rmk->rck", hit_table.astype(bf16), fresh, preferred_element_type=f32
    ).astype(bf16)
    cache_keys = jnp.where(jnp.any(hit_table, axis=2)[:, :, None], placed, cache_part[..., :HD])
    keys = jnp.concatenate([cache_keys, step_part[..., :HD]], axis=1)
    values = jnp.concatenate([cache_part[..., HD:], step_part[..., HD:]], axis=1)
    heads = query_pack.reshape(seq_count, req_rows, tok_rows, groups, HD).transpose(1, 3, 0, 2, 4)
    heads = heads.reshape(req_rows, groups, step_total, HD)
    scores = jnp.einsum("rgqd,rnd->rgqn", heads, keys, preferred_element_type=f32) * HD ** (-0.5)
    cache_allowed = (positions[None] >= cache_spans[:, 0:1]) & (positions[None] < cache_spans[:, 1:2])
    step_allowed = jnp.arange(step_total)[None, :] <= jnp.arange(step_total)[:, None]
    allowed = jnp.concatenate(
        [
            jnp.broadcast_to(cache_allowed[:, None, :], (req_rows, step_total, cache_total)),
            jnp.broadcast_to(step_allowed[None], (req_rows, step_total, step_total)),
        ],
        axis=2,
    )
    scores = jnp.where(allowed[:, None], scores, NEG)
    exps = jnp.exp(scores - jnp.max(scores, axis=-1, keepdims=True))
    totals = jnp.sum(exps, axis=-1, keepdims=True)
    mixed = jnp.einsum("rgqn,rnd->rgqd", exps.astype(bf16), values, preferred_element_type=f32)
    mixed = (mixed / totals).astype(bf16)
    mixed = mixed.reshape(req_rows, groups, seq_count, tok_rows, HD).transpose(2, 0, 3, 1, 4)
    mixed = mixed.reshape(seq_count, req_rows, tok_rows, groups * HD)
    mixed = lax.all_to_all(mixed, "seq", split_axis=0, concat_axis=0, tiled=True)
    attended = mixed.transpose(1, 2, 0, 3).reshape(req_rows * tok_rows, model_width)
    attended_f = attended.astype(f32)
    mean_square = jnp.mean(attended_f * attended_f, axis=-1, keepdims=True)
    normed = (attended_f * lax.rsqrt(mean_square + 1e-06) * norm_gain).astype(bf16)
    tokens = lax.all_gather(normed, "req", axis=0, tiled=True)
    all_routes = lax.all_gather(routes.reshape(req_rows * tok_rows, TOP), "req", axis=0, tiled=True)
    all_weights = lax.all_gather(
        route_weights.reshape(req_rows * tok_rows, TOP), "req", axis=0, tiled=True
    )
    mine = req_index * local_experts + jnp.arange(local_experts)
    share = jnp.sum(
        jnp.where(all_routes[:, :, None] == mine[None, None], all_weights[:, :, None], 0.0), axis=1
    )
    total = jnp.zeros(tokens.shape, f32)
    for e in range(local_experts):
        hidden = jnp.dot(tokens, expert_gate_up[e], preferred_element_type=f32)
        active = (jax.nn.silu(hidden[:, :FF]) * hidden[:, FF:]).astype(bf16)
        result = jnp.dot(active, expert_down[e], preferred_element_type=f32).astype(bf16)
        total = total + result.astype(f32) * share[:, e : e + 1]
    pieces = total.astype(bf16).reshape(owner_count, req_rows * tok_rows, model_width)
    pieces = lax.all_to_all(pieces, "req", split_axis=0, concat_axis=0, tiled=True)
    mixture = jnp.sum(pieces.astype(f32), axis=0)
    return (attended_f + mixture).astype(bf16).reshape(req_rows, tok_rows, model_width)


def solution(mesh):
    body = head_parallel_body if mesh.shape["seq"] == KVH else body_wide
    in_specs = (
        P("req", "seq", None),
        P(None, "req", "seq", None),
        P(None, "req", "seq", None),
        P("req", None),
        P("req", None),
        P("req", "seq", None),
        P(),
        P(),
        P("req", "seq", None),
        P("req", "seq", None),
        P("req", None, None),
        P("req", None, None),
    )
    out_specs = P("req", "seq", None)
    return jax.shard_map(body, mesh=mesh, in_specs=in_specs, out_specs=out_specs, check_vma=False)
```

```python
import jax
import jax.numpy as jnp
from jax import lax
from jax.experimental import pallas as pl
from jax.experimental.pallas import tpu as pltpu
from jax.sharding import PartitionSpec as P

H = 24
KVH = 8
HD = 64
FF = 512
TOP = 8
CAP = 16


NEG = -1e30
THETA = 10000.0


def rotate(key_heads, positions):
    half_dim = key_heads.shape[-1] // 2
    exponent = jnp.arange(half_dim).astype(jnp.float32) * (2.0 / key_heads.shape[-1])
    inverse = THETA ** (-exponent)
    angles = positions.astype(jnp.float32)[..., None] * inverse
    cosine = jnp.cos(angles)[..., None, :]
    sine_part = jnp.sin(angles)[..., None, :]
    lower_half = key_heads[..., :half_dim]
    upper_half = key_heads[..., half_dim:]
    return jnp.concatenate(
        [
            lower_half * cosine - upper_half * sine_part,
            upper_half * cosine + lower_half * sine_part,
        ],
        axis=-1,
    )


def partial_attend(packed):
    query_rows, key_rows, value_rows, allowed = packed
    query_count, model_width = query_rows.shape
    key_count = key_rows.shape[0]
    groups = H // KVH
    query_heads = query_rows.reshape(query_count, KVH, groups, HD)
    key_heads = key_rows.reshape(key_count, KVH, HD)
    value_heads = value_rows.reshape(key_count, KVH, HD)
    scores = jnp.einsum(
        "qkgd,nkd->kgqn", query_heads, key_heads, preferred_element_type=jnp.float32
    ) * HD ** (-0.5)
    scores = jnp.where(allowed[None, None, :, :], scores, NEG)
    highest = jnp.max(scores, axis=-1, keepdims=True)
    exps = jnp.exp(scores - highest)
    totals = jnp.sum(exps, axis=-1)
    weights = exps.astype(jnp.bfloat16)
    mixed_rows = jnp.einsum(
        "kgqn,nkd->qkgd", weights, value_heads, preferred_element_type=jnp.float32
    )
    mixed_rows = mixed_rows / jnp.transpose(totals, (2, 0, 1))[..., None]
    log_total = highest[..., 0] + jnp.log(totals)
    log_rows = jnp.transpose(log_total, (2, 0, 1)).reshape(query_count, H)
    return (mixed_rows.reshape(query_count, model_width), log_rows)


def body_wide(
    queries,
    new_kv,
    cache_kv,
    cache_spans,
    recompute_rows,
    held_states,
    key_weight,
    norm_gain,
    routes,
    route_weights,
    expert_gate_up,
    expert_down,
):
    seq_index = lax.axis_index("seq")
    seq_count = lax.axis_size("seq")
    owner_count = lax.axis_size("req")
    req_rows, tok_rows, model_width = queries.shape
    cache_rows = cache_kv.shape[2]
    held_rows = held_states.shape[1]
    local_experts = expert_gate_up.shape[0]
    expert_total = owner_count * local_experts
    my_positions = lax.dynamic_slice_in_dim(recompute_rows, seq_index * held_rows, held_rows, 1)
    projected = jnp.dot(
        held_states.reshape(req_rows * held_rows, model_width),
        key_weight,
        preferred_element_type=jnp.float32,
    )
    rotated = rotate(projected.reshape(req_rows, held_rows, KVH, HD), my_positions)
    rotated = rotated.reshape(req_rows, held_rows, KVH * HD).astype(jnp.bfloat16)
    fresh_rows = lax.all_gather(rotated, "seq", axis=1, tiled=True)
    cache_positions = seq_index * cache_rows + jnp.arange(cache_rows)
    hit_table = recompute_rows[:, None, :] == cache_positions[None, :, None]
    placed = jnp.einsum(
        "rcm,rmk->rck",
        hit_table.astype(jnp.bfloat16),
        fresh_rows,
        preferred_element_type=jnp.float32,
    ).astype(jnp.bfloat16)
    cache_keys = jnp.where(jnp.any(hit_table, axis=2)[:, :, None], placed, cache_kv[0])
    span_start = cache_spans[:, 0:1]
    span_end = cache_spans[:, 1:2]
    all_queries = lax.all_gather(queries, "seq", axis=1, tiled=True)
    step_total = all_queries.shape[1]
    cache_allowed = (cache_positions[None, :] >= span_start) & (cache_positions[None, :] < span_end)
    key_positions = seq_index * tok_rows + jnp.arange(tok_rows)
    step_allowed = key_positions[None, :] <= jnp.arange(step_total)[:, None]
    allowed = jnp.concatenate(
        [
            jnp.broadcast_to(cache_allowed[:, None, :], (req_rows, step_total, cache_rows)),
            jnp.broadcast_to(step_allowed[None], (req_rows, step_total, tok_rows)),
        ],
        axis=2,
    )
    key_rows = jnp.concatenate([cache_keys, new_kv[0]], axis=1)
    value_rows = jnp.concatenate([cache_kv[1], new_kv[1]], axis=1)
    part_out, part_log = lax.map(partial_attend, (all_queries, key_rows, value_rows, allowed))
    piece_out, piece_log = (
        lax.all_to_all(part_out[None], "seq", split_axis=2, concat_axis=0, tiled=True),
        lax.all_to_all(part_log[None], "seq", split_axis=2, concat_axis=0, tiled=True),
    )
    best_log = jnp.max(piece_log, axis=0)
    factors = jnp.exp(piece_log - best_log[None])
    factor_sum = jnp.sum(factors, axis=0)
    spread_out = piece_out.reshape(seq_count, req_rows, tok_rows, H, HD)
    combined = jnp.sum(spread_out * factors[..., None], axis=0) / factor_sum[..., None]
    attended_f = combined.reshape(req_rows, tok_rows, model_width)
    attended = attended_f.astype(jnp.bfloat16)
    attended_f = attended.astype(jnp.float32)
    mean_square = jnp.mean(attended_f * attended_f, axis=-1, keepdims=True)
    normed = (attended_f * lax.rsqrt(mean_square + 1e-06) * norm_gain).astype(jnp.bfloat16)
    route_flat = routes.reshape(req_rows, tok_rows * TOP)
    expert_match = (route_flat[:, :, None] == jnp.arange(expert_total)[None, None, :]).astype(
        jnp.int32
    )
    earlier = jnp.cumsum(expert_match, axis=1) - expert_match
    slot_index = jnp.sum(earlier * expert_match, axis=2)
    target = route_flat * CAP + slot_index
    slot_match = target[:, :, None] == jnp.arange(expert_total * CAP)[None, None, :]
    dispatch = jnp.any(
        slot_match.reshape(req_rows, tok_rows, TOP, expert_total * CAP), axis=2
    ).astype(jnp.bfloat16)
    dispatch = dispatch.reshape(req_rows, tok_rows, owner_count, local_experts, CAP)
    outgoing = jnp.einsum(
        "rtnec,rtd->nrecd", dispatch, normed, preferred_element_type=jnp.float32
    ).astype(jnp.bfloat16)
    hidden = jnp.einsum(
        "srecd,edf->srecf",
        lax.all_to_all(outgoing, "req", split_axis=0, concat_axis=0, tiled=True),
        expert_gate_up,
        preferred_element_type=jnp.float32,
    )
    active = (jax.nn.silu(hidden[..., :FF]) * hidden[..., FF:]).astype(jnp.bfloat16)
    result = jnp.einsum(
        "srecf,efd->srecd", active, expert_down, preferred_element_type=jnp.float32
    ).astype(jnp.bfloat16)
    returned = lax.all_to_all(result, "req", split_axis=0, concat_axis=0, tiled=True)
    owner_of = route_flat // local_experts
    local_of = route_flat % local_experts
    flat_index = (
        (owner_of * req_rows + jnp.arange(req_rows)[:, None]) * local_experts + local_of
    ) * CAP + slot_index
    returned_rows = jnp.take(returned.reshape(-1, model_width), flat_index.reshape(-1), axis=0)
    returned_rows = returned_rows.reshape(req_rows, tok_rows, TOP, model_width)
    mixture = jnp.einsum(
        "rtk,rtkd->rtd",
        route_weights,
        returned_rows.astype(jnp.float32),
        precision=lax.Precision.HIGHEST,
    )
    return (attended_f + mixture).astype(jnp.bfloat16)


def layer_kernel(
    spans_ref,
    rec_ref,
    cos_ref,
    sin_ref,
    q_ref,
    new_ref,
    cache_ref,
    held_ref,
    kw_ref,
    gain_ref,
    routes_ref,
    rw_ref,
    gu_hbm,
    dn_hbm,
    out_ref,
    gu_v,
    dn_v,
    kvsend,
    stsend,
    qsend,
    fsend,
    osend,
    crecv,
    srecv,
    qrecv,
    frecv,
    orecv,
    kbuf,
    vbuf,
    att,
    trecv,
    wrecv,
    total,
    psend,
    precv,
    load_sem,
    s_sem,
    r_sem,
    zs_sem,
    zr_sem,
):
    bf16 = jnp.bfloat16
    f32 = jnp.float32
    me = lax.axis_index("seq")
    S = lax.axis_size("seq")
    mz = lax.axis_index("req")
    N = lax.axis_size("req")
    groups = H // KVH
    tok = q_ref.shape[1]
    crows = cache_ref.shape[2]
    held = frecv.shape[0] // S
    width = q_ref.shape[2]
    local_experts = gu_v.shape[0]
    ctotal = S * crows
    stotal = S * tok

    barrier = pltpu.get_barrier_semaphore()
    for k in range(1, S):
        pl.semaphore_signal(barrier, inc=1, device_id={"seq": lax.rem(me + k, S)})
    for k in range(1, N):
        pl.semaphore_signal(barrier, inc=1, device_id={"req": lax.rem(mz + k, N)})

    def lanes(rows):
        return lax.broadcasted_iota(jnp.int32, (rows, 2 * HD), 1)

    def join(low, low_roll, high, high_roll, scale=None):
        a, b = low.astype(f32), high.astype(f32)
        a = pltpu.roll(a, HD, 1) if low_roll else a
        b = pltpu.roll(b, HD, 1) if high_roll else b
        c = jnp.where(lanes(a.shape[0]) < HD, a, b)
        return (c if scale is None else c * scale).astype(bf16)

    for h in range(KVH):
        cols = slice((h // 2) * 2 * HD, (h // 2 + 1) * 2 * HD)
        odd = h % 2 == 1
        for g in range(groups):
            c = h * groups + g
            qc = slice((c // 2) * 2 * HD, (c // 2 + 1) * 2 * HD)
            qsend[h, g] = join(q_ref[0, :, qc], c % 2 == 1, q_ref[1, :, qc], c % 2 == 0, HD**-0.5)
        for src, dst in ((cache_ref, kvsend), (new_ref, stsend)):
            dst[h, 0] = join(src[0, 0, :, cols], odd, src[1, 0, :, cols], not odd)
            dst[h, 1] = join(src[1, 1, :, cols], odd, src[0, 1, :, cols], not odd)

    def row_at(i, n):
        return pl.ds(pl.multiple_of(i * n, n), n)

    def exchange(kind, k, slot):
        peer = lax.rem(me + k, S)
        src, dst = (
            (qsend.at[peer], qrecv.at[:, row_at(slot, tok), :]),
            (stsend.at[peer], srecv.at[:, row_at(slot, tok), :]),
            (kvsend.at[peer, 0], crecv.at[0, row_at(slot, crows), :]),
            (kvsend.at[peer, 1], crecv.at[1, row_at(slot, crows), :]),
            (fsend.at[peer], frecv.at[row_at(slot, held), :]),
            (osend.at[:, row_at(peer, tok), :], orecv.at[slot]),
        )[kind]
        return pltpu.make_async_remote_copy(
            src_ref=src,
            dst_ref=dst,
            send_sem=s_sem.at[kind, k],
            recv_sem=r_sem.at[kind, k],
            device_id={"seq": peer},
        )

    def arrive(kind):
        for k in range(1, S):
            exchange(kind, k, lax.rem(me + S - k, S)).wait_recv()

    pl.semaphore_wait(barrier, S - 1 + N - 1)
    for k in range(1, S):
        for kind in (0, 1, 2):
            exchange(kind, k, me).start()

    loads = []
    for e in range(local_experts):
        loads.append(pltpu.make_async_copy(gu_hbm.at[e], gu_v.at[e], load_sem.at[0, e]))
        loads.append(pltpu.make_async_copy(dn_hbm.at[e], dn_v.at[e], load_sem.at[1, e]))

    fresh = jnp.dot(held_ref[...], kw_ref[...], preferred_element_type=f32)
    low_part = lax.broadcasted_iota(jnp.int32, fresh.shape, 1) % HD < HD // 2
    partner = jnp.where(
        low_part,
        pltpu.roll(fresh, fresh.shape[1] - HD // 2, 1),
        pltpu.roll(fresh, HD // 2, 1),
    )
    fresh = fresh * jnp.tile(cos_ref[...], (1, KVH // 2)) + partner * jnp.tile(
        sin_ref[...], (1, KVH // 2)
    )
    for h in range(KVH):
        cols = slice((h // 2) * 2 * HD, (h // 2 + 1) * 2 * HD)
        odd = h % 2 == 1
        fsend[h] = join(fresh[:held, cols], odd, fresh[held:, cols], not odd)
    for k in range(1, S):
        exchange(4, k, me).start()
    for k in range(1, S):
        exchange(3, k, me).start()
    for load in loads:
        load.start()

    qrecv[:, row_at(me, tok), :] = qsend[me]
    srecv[:, row_at(me, tok), :] = stsend[me]
    crecv[:, row_at(me, crows), :] = kvsend[me]
    frecv[row_at(me, held), :] = fsend[me]

    expert_lane = lax.broadcasted_iota(jnp.int32, (2 * tok, 128), 1)
    dense = jnp.zeros((2 * tok, 128), f32)
    for k in range(TOP):
        dense = dense + jnp.where(routes_ref[:, k : k + 1] == expert_lane, rw_ref[:, k : k + 1], 0.0)
    wrecv[mz] = dense

    def across(kind, k, slot):
        peer = lax.rem(mz + k, N)
        src, dst = (
            (wrecv.at[mz], wrecv.at[slot]),
            (trecv.at[mz], trecv.at[slot]),
            (psend.at[peer], precv.at[slot]),
        )[kind]
        return pltpu.make_async_remote_copy(
            src_ref=src,
            dst_ref=dst,
            send_sem=zs_sem.at[kind, k],
            recv_sem=zr_sem.at[kind, k],
            device_id={"req": peer},
        )

    def across_arrive(kind):
        for k in range(1, N):
            across(kind, k, lax.rem(mz + N - k, N)).wait_recv()

    for k in range(1, N):
        across(0, k, mz).start()

    for kind in (0, 1, 2, 4):
        arrive(kind)
    for r in range(2):
        if r == 1:
            arrive(3)
        key_half = (lanes(crows) < HD) if r == 0 else (lanes(crows) >= HD)
        ones = jnp.ones((S * held, 2 * HD), bf16)
        spread = jnp.concatenate([frecv[...], ones], axis=1)
        wanted = rec_ref[r : r + 1, :]

        def place(i, carry):
            rows = row_at(i, crows)
            kv = crecv[r, rows, :].astype(f32)
            where_to = lax.broadcasted_iota(jnp.int32, (crows, S * held), 0) + i * crows
            hit = jnp.where(where_to == wanted, 1.0, 0.0).astype(bf16)
            both = jnp.dot(hit, spread, preferred_element_type=f32)
            keys = jnp.where(both[:, 2 * HD :] > 0.5, both[:, : 2 * HD], kv)
            kbuf[rows, :] = jnp.where(key_half, keys, 0.0).astype(bf16)
            vbuf[rows, :] = jnp.where(key_half, 1.0, kv).astype(bf16)
            return carry

        lax.fori_loop(0, S, place, 0)
        step = srecv[r].astype(f32)
        step_half = (lanes(stotal) < HD) if r == 0 else (lanes(stotal) >= HD)
        kbuf[ctotal:, :] = jnp.where(step_half, step, 0.0).astype(bf16)
        vbuf[ctotal:, :] = jnp.where(step_half, 1.0, step).astype(bf16)
        position = lax.broadcasted_iota(jnp.int32, (1, ctotal), 1)
        open_row = (position >= spans_ref[r, 0]) & (position < spans_ref[r, 1])
        bias = jnp.where(open_row, 0.0, NEG)
        causal = lax.broadcasted_iota(jnp.int32, (stotal, stotal), 1) <= lax.broadcasted_iota(
            jnp.int32, (stotal, stotal), 0
        )
        contract = (((1,), (1,)), ((), ()))

        def attend(g, carry):
            query = qrecv[g]
            old = lax.dot_general(
                query, kbuf[:ctotal, :], contract, preferred_element_type=f32
            ) + bias
            new = lax.dot_general(query, kbuf[ctotal:, :], contract, preferred_element_type=f32)
            new = jnp.where(causal, new, NEG)
            highest = jnp.maximum(
                jnp.max(old, axis=-1, keepdims=True), jnp.max(new, axis=-1, keepdims=True)
            )
            mixed = jnp.dot(
                jnp.exp(old - highest).astype(bf16), vbuf[:ctotal, :], preferred_element_type=f32
            ) + jnp.dot(
                jnp.exp(new - highest).astype(bf16), vbuf[ctotal:, :], preferred_element_type=f32
            )
            mixed = mixed / pltpu.roll(mixed, HD, 1)
            if r == 0:
                osend[g] = mixed.astype(bf16)
            else:
                osend[g] = jnp.where(
                    lanes(stotal) < HD, mixed, osend[g].astype(f32)
                ).astype(bf16)
            return carry

        lax.fori_loop(0, groups, attend, 0)

    for k in range(1, S):
        exchange(5, k, me).start()
    orecv[me] = osend[:, row_at(me, tok), :]
    arrive(5)
    for pair in range(H // 2):
        first, second = 2 * pair, 2 * pair + 1
        one = orecv[first // groups, first % groups]
        two = orecv[second // groups, second % groups]
        cols = slice(pair * 2 * HD, (pair + 1) * 2 * HD)
        att[:tok, cols] = join(one, True, two, False)
        att[tok:, cols] = join(one, False, two, True)
    attended = att[...].astype(f32)
    mean_square = jnp.mean(attended * attended, axis=-1, keepdims=True)
    trecv[mz] = (attended * lax.rsqrt(mean_square + 1e-06) * gain_ref[...]).astype(bf16)
    for k in range(1, N):
        across(1, k, mz).start()
    across_arrive(0)
    for load in loads:
        load.wait()
    across_arrive(1)

    tokens_total = N * 2 * tok
    total[...] = jnp.zeros_like(total)

    def expert(e, carry):
        tokens = trecv[...].reshape(tokens_total, width)
        hidden = jnp.dot(tokens, gu_v[e], preferred_element_type=f32)
        gate, up = hidden[:, :FF], hidden[:, FF:]
        active = (gate / (1.0 + jnp.exp(-gate)) * up).astype(bf16)
        result = jnp.dot(active, dn_v[e], preferred_element_type=f32).astype(bf16)
        weights = wrecv[...].reshape(tokens_total, 128)
        lane = lax.broadcasted_iota(jnp.int32, weights.shape, 1)
        share = jnp.sum(
            jnp.where(lane == mz * local_experts + e, weights, 0.0), axis=1, keepdims=True
        )
        total[...] += result.astype(f32) * share
        return carry

    lax.fori_loop(0, local_experts, expert, 0)
    psend[...] = total[...].astype(bf16).reshape(psend.shape)
    for k in range(1, N):
        across(2, k, mz).start()
    mixture = att[...].astype(f32) + psend[mz].astype(f32)
    across_arrive(2)
    for k in range(1, N):
        mixture = mixture + precv[lax.rem(mz + N - k, N)].astype(f32)
    out_ref[...] = mixture.astype(bf16)
    for kind in range(6):
        for k in range(1, S):
            exchange(kind, k, me).wait_send()
    for kind in range(3):
        for k in range(1, N):
            across(kind, k, mz).wait_send()


def head_parallel_body(
    queries,
    new_kv,
    cache_kv,
    cache_spans,
    recompute_rows,
    held_states,
    key_weight,
    norm_gain,
    routes,
    route_weights,
    expert_gate_up,
    expert_down,
):
    seq_index = lax.axis_index("seq")
    S = lax.axis_size("seq")
    N = lax.axis_size("req")
    req_rows, tok, width = queries.shape
    crows = cache_kv.shape[2]
    held = held_states.shape[1]
    local_experts = expert_gate_up.shape[0]
    groups = H // KVH
    bf16, f32 = jnp.bfloat16, jnp.float32
    positions = lax.dynamic_slice_in_dim(recompute_rows, seq_index * held, held, 1)
    half = HD // 2
    inverse = THETA ** (-(jnp.arange(half).astype(f32) * (2.0 / HD)))
    angles = positions.reshape(req_rows * held, 1).astype(f32) * inverse
    cosine, sine = jnp.cos(angles), jnp.sin(angles)
    cos_table = jnp.concatenate([cosine] * 4, axis=1)
    sin_table = jnp.concatenate([-sine, sine, -sine, sine], axis=1)
    vmem = pl.BlockSpec(memory_space=pltpu.VMEM)
    smem = pl.BlockSpec(memory_space=pltpu.SMEM)
    hbm = pl.BlockSpec(memory_space=pl.ANY)
    lane = 2 * HD
    rows = req_rows * tok
    out = pl.pallas_call(
        layer_kernel,
        out_shape=jax.ShapeDtypeStruct((rows, width), bf16),
        in_specs=[smem] + [vmem] * 11 + [hbm, hbm],
        out_specs=vmem,
        scratch_shapes=[
            pltpu.VMEM(expert_gate_up.shape, bf16),
            pltpu.VMEM(expert_down.shape, bf16),
            pltpu.VMEM((S, 2, crows, lane), bf16),
            pltpu.VMEM((S, 2, tok, lane), bf16),
            pltpu.VMEM((S, groups, tok, lane), bf16),
            pltpu.VMEM((S, held, lane), bf16),
            pltpu.VMEM((groups, S * tok, lane), bf16),
            pltpu.VMEM((2, S * crows, lane), bf16),
            pltpu.VMEM((2, S * tok, lane), bf16),
            pltpu.VMEM((groups, S * tok, lane), bf16),
            pltpu.VMEM((S * held, lane), bf16),
            pltpu.VMEM((S, groups, tok, lane), bf16),
            pltpu.VMEM((S * (crows + tok), lane), bf16),
            pltpu.VMEM((S * (crows + tok), lane), bf16),
            pltpu.VMEM((rows, width), bf16),
            pltpu.VMEM((N, rows, width), bf16),
            pltpu.VMEM((N, rows, 128), f32),
            pltpu.VMEM((N * rows, width), f32),
            pltpu.VMEM((N, rows, width), bf16),
            pltpu.VMEM((N, rows, width), bf16),
            pltpu.SemaphoreType.DMA((2, local_experts)),
            pltpu.SemaphoreType.DMA((6, S)),
            pltpu.SemaphoreType.DMA((6, S)),
            pltpu.SemaphoreType.DMA((3, N)),
            pltpu.SemaphoreType.DMA((3, N)),
        ],
        compiler_params=pltpu.CompilerParams(
            collective_id=0, has_side_effects=True, vmem_limit_bytes=60 << 20
        ),
        name="layer",
    )(
        cache_spans,
        recompute_rows,
        cos_table,
        sin_table,
        queries,
        new_kv,
        cache_kv,
        held_states.reshape(req_rows * held, width),
        key_weight,
        norm_gain.reshape(1, width),
        routes.reshape(rows, TOP),
        route_weights.reshape(rows, TOP),
        expert_gate_up,
        expert_down,
    )
    return out.reshape(req_rows, tok, width)


def solution(mesh):
    body = head_parallel_body if mesh.shape["seq"] == KVH else body_wide
    in_specs = (
        P("req", "seq", None),
        P(None, "req", "seq", None),
        P(None, "req", "seq", None),
        P("req", None),
        P("req", None),
        P("req", "seq", None),
        P(),
        P(),
        P("req", "seq", None),
        P("req", "seq", None),
        P("req", None, None),
        P("req", None, None),
    )
    out_specs = P("req", "seq", None)
    return jax.shard_map(body, mesh=mesh, in_specs=in_specs, out_specs=out_specs, check_vma=False)
```

```python
import jax
import jax.numpy as jnp
from jax import lax
from jax.experimental import pallas as pl
from jax.experimental.pallas import tpu as pltpu
from jax.sharding import PartitionSpec as P

H = 24
KVH = 8
HD = 64
FF = 512
TOP = 8
CAP = 16


NEG = -1e30
THETA = 10000.0


def rotate(key_heads, positions):
    half_dim = key_heads.shape[-1] // 2
    exponent = jnp.arange(half_dim).astype(jnp.float32) * (2.0 / key_heads.shape[-1])
    inverse = THETA ** (-exponent)
    angles = positions.astype(jnp.float32)[..., None] * inverse
    cosine = jnp.cos(angles)[..., None, :]
    sine_part = jnp.sin(angles)[..., None, :]
    lower_half = key_heads[..., :half_dim]
    upper_half = key_heads[..., half_dim:]
    return jnp.concatenate(
        [
            lower_half * cosine - upper_half * sine_part,
            upper_half * cosine + lower_half * sine_part,
        ],
        axis=-1,
    )


def partial_attend(packed):
    query_rows, key_rows, value_rows, allowed = packed
    query_count, model_width = query_rows.shape
    key_count = key_rows.shape[0]
    groups = H // KVH
    query_heads = query_rows.reshape(query_count, KVH, groups, HD)
    key_heads = key_rows.reshape(key_count, KVH, HD)
    value_heads = value_rows.reshape(key_count, KVH, HD)
    scores = jnp.einsum(
        "qkgd,nkd->kgqn", query_heads, key_heads, preferred_element_type=jnp.float32
    ) * HD ** (-0.5)
    scores = jnp.where(allowed[None, None, :, :], scores, NEG)
    highest = jnp.max(scores, axis=-1, keepdims=True)
    exps = jnp.exp(scores - highest)
    totals = jnp.sum(exps, axis=-1)
    weights = exps.astype(jnp.bfloat16)
    mixed_rows = jnp.einsum(
        "kgqn,nkd->qkgd", weights, value_heads, preferred_element_type=jnp.float32
    )
    mixed_rows = mixed_rows / jnp.transpose(totals, (2, 0, 1))[..., None]
    log_total = highest[..., 0] + jnp.log(totals)
    log_rows = jnp.transpose(log_total, (2, 0, 1)).reshape(query_count, H)
    return (mixed_rows.reshape(query_count, model_width), log_rows)


def body_wide(
    queries,
    new_kv,
    cache_kv,
    cache_spans,
    recompute_rows,
    held_states,
    key_weight,
    norm_gain,
    routes,
    route_weights,
    expert_gate_up,
    expert_down,
):
    seq_index = lax.axis_index("seq")
    seq_count = lax.axis_size("seq")
    owner_count = lax.axis_size("req")
    req_rows, tok_rows, model_width = queries.shape
    cache_rows = cache_kv.shape[2]
    held_rows = held_states.shape[1]
    local_experts = expert_gate_up.shape[0]
    expert_total = owner_count * local_experts
    my_positions = lax.dynamic_slice_in_dim(recompute_rows, seq_index * held_rows, held_rows, 1)
    projected = jnp.dot(
        held_states.reshape(req_rows * held_rows, model_width),
        key_weight,
        preferred_element_type=jnp.float32,
    )
    rotated = rotate(projected.reshape(req_rows, held_rows, KVH, HD), my_positions)
    rotated = rotated.reshape(req_rows, held_rows, KVH * HD).astype(jnp.bfloat16)
    fresh_rows = lax.all_gather(rotated, "seq", axis=1, tiled=True)
    cache_positions = seq_index * cache_rows + jnp.arange(cache_rows)
    hit_table = recompute_rows[:, None, :] == cache_positions[None, :, None]
    placed = jnp.einsum(
        "rcm,rmk->rck",
        hit_table.astype(jnp.bfloat16),
        fresh_rows,
        preferred_element_type=jnp.float32,
    ).astype(jnp.bfloat16)
    cache_keys = jnp.where(jnp.any(hit_table, axis=2)[:, :, None], placed, cache_kv[0])
    span_start = cache_spans[:, 0:1]
    span_end = cache_spans[:, 1:2]
    all_queries = lax.all_gather(queries, "seq", axis=1, tiled=True)
    step_total = all_queries.shape[1]
    cache_allowed = (cache_positions[None, :] >= span_start) & (cache_positions[None, :] < span_end)
    key_positions = seq_index * tok_rows + jnp.arange(tok_rows)
    step_allowed = key_positions[None, :] <= jnp.arange(step_total)[:, None]
    allowed = jnp.concatenate(
        [
            jnp.broadcast_to(cache_allowed[:, None, :], (req_rows, step_total, cache_rows)),
            jnp.broadcast_to(step_allowed[None], (req_rows, step_total, tok_rows)),
        ],
        axis=2,
    )
    key_rows = jnp.concatenate([cache_keys, new_kv[0]], axis=1)
    value_rows = jnp.concatenate([cache_kv[1], new_kv[1]], axis=1)
    part_out, part_log = lax.map(partial_attend, (all_queries, key_rows, value_rows, allowed))
    piece_out, piece_log = (
        lax.all_to_all(part_out[None], "seq", split_axis=2, concat_axis=0, tiled=True),
        lax.all_to_all(part_log[None], "seq", split_axis=2, concat_axis=0, tiled=True),
    )
    best_log = jnp.max(piece_log, axis=0)
    factors = jnp.exp(piece_log - best_log[None])
    factor_sum = jnp.sum(factors, axis=0)
    spread_out = piece_out.reshape(seq_count, req_rows, tok_rows, H, HD)
    combined = jnp.sum(spread_out * factors[..., None], axis=0) / factor_sum[..., None]
    attended_f = combined.reshape(req_rows, tok_rows, model_width)
    attended = attended_f.astype(jnp.bfloat16)
    attended_f = attended.astype(jnp.float32)
    mean_square = jnp.mean(attended_f * attended_f, axis=-1, keepdims=True)
    normed = (attended_f * lax.rsqrt(mean_square + 1e-06) * norm_gain).astype(jnp.bfloat16)
    route_flat = routes.reshape(req_rows, tok_rows * TOP)
    expert_match = (route_flat[:, :, None] == jnp.arange(expert_total)[None, None, :]).astype(
        jnp.int32
    )
    earlier = jnp.cumsum(expert_match, axis=1) - expert_match
    slot_index = jnp.sum(earlier * expert_match, axis=2)
    target = route_flat * CAP + slot_index
    slot_match = target[:, :, None] == jnp.arange(expert_total * CAP)[None, None, :]
    dispatch = jnp.any(
        slot_match.reshape(req_rows, tok_rows, TOP, expert_total * CAP), axis=2
    ).astype(jnp.bfloat16)
    dispatch = dispatch.reshape(req_rows, tok_rows, owner_count, local_experts, CAP)
    outgoing = jnp.einsum(
        "rtnec,rtd->nrecd", dispatch, normed, preferred_element_type=jnp.float32
    ).astype(jnp.bfloat16)
    hidden = jnp.einsum(
        "srecd,edf->srecf",
        lax.all_to_all(outgoing, "req", split_axis=0, concat_axis=0, tiled=True),
        expert_gate_up,
        preferred_element_type=jnp.float32,
    )
    active = (jax.nn.silu(hidden[..., :FF]) * hidden[..., FF:]).astype(jnp.bfloat16)
    result = jnp.einsum(
        "srecf,efd->srecd", active, expert_down, preferred_element_type=jnp.float32
    ).astype(jnp.bfloat16)
    returned = lax.all_to_all(result, "req", split_axis=0, concat_axis=0, tiled=True)
    owner_of = route_flat // local_experts
    local_of = route_flat % local_experts
    flat_index = (
        (owner_of * req_rows + jnp.arange(req_rows)[:, None]) * local_experts + local_of
    ) * CAP + slot_index
    returned_rows = jnp.take(returned.reshape(-1, model_width), flat_index.reshape(-1), axis=0)
    returned_rows = returned_rows.reshape(req_rows, tok_rows, TOP, model_width)
    mixture = jnp.einsum(
        "rtk,rtkd->rtd",
        route_weights,
        returned_rows.astype(jnp.float32),
        precision=lax.Precision.HIGHEST,
    )
    return (attended_f + mixture).astype(jnp.bfloat16)


def layer_kernel(
    spans_ref,
    rec_ref,
    cos_ref,
    sin_ref,
    q_ref,
    new_ref,
    cache_ref,
    held_ref,
    kw_ref,
    gain_ref,
    routes_ref,
    rw_ref,
    gu_hbm,
    dn_hbm,
    out_ref,
    gu_v,
    dn_v,
    kvsend,
    stsend,
    qsend,
    fsend,
    osend,
    crecv,
    srecv,
    qrecv,
    frecv,
    orecv,
    kbuf,
    vbuf,
    att,
    trecv,
    wrecv,
    total,
    psend,
    precv,
    load_sem,
    s_sem,
    r_sem,
    zs_sem,
    zr_sem,
    ts_sem,
    tr_sem,
):
    bf16 = jnp.bfloat16
    f32 = jnp.float32
    me = lax.axis_index("seq")
    S = lax.axis_size("seq")
    mz = lax.axis_index("req")
    N = lax.axis_size("req")
    groups = H // KVH
    tok = q_ref.shape[1]
    crows = cache_ref.shape[2]
    held = frecv.shape[0] // S
    width = q_ref.shape[2]
    local_experts = gu_v.shape[0]
    ctotal = S * crows
    stotal = S * tok

    barrier = pltpu.get_barrier_semaphore()
    for k in range(1, S):
        pl.semaphore_signal(barrier, inc=1, device_id={"seq": lax.rem(me + k, S)})
    for k in range(1, N):
        pl.semaphore_signal(barrier, inc=1, device_id={"req": lax.rem(mz + k, N)})

    def lanes(rows):
        return lax.broadcasted_iota(jnp.int32, (rows, 2 * HD), 1)

    def join(low, low_roll, high, high_roll, scale=None):
        a, b = low.astype(f32), high.astype(f32)
        a = pltpu.roll(a, HD, 1) if low_roll else a
        b = pltpu.roll(b, HD, 1) if high_roll else b
        c = jnp.where(lanes(a.shape[0]) < HD, a, b)
        return (c if scale is None else c * scale).astype(bf16)

    for h in range(KVH):
        cols = slice((h // 2) * 2 * HD, (h // 2 + 1) * 2 * HD)
        odd = h % 2 == 1
        for g in range(groups):
            c = h * groups + g
            qc = slice((c // 2) * 2 * HD, (c // 2 + 1) * 2 * HD)
            qsend[h, g] = join(q_ref[0, :, qc], c % 2 == 1, q_ref[1, :, qc], c % 2 == 0, HD**-0.5)
        for src, dst in ((cache_ref, kvsend), (new_ref, stsend)):
            dst[h, 0] = join(src[0, 0, :, cols], odd, src[1, 0, :, cols], not odd)
            dst[h, 1] = join(src[1, 1, :, cols], odd, src[0, 1, :, cols], not odd)

    def row_at(i, n):
        return pl.ds(pl.multiple_of(i * n, n), n)

    def exchange(kind, k, slot):
        peer = lax.rem(me + k, S)
        src, dst = (
            (qsend.at[peer], qrecv.at[:, row_at(slot, tok), :]),
            (stsend.at[peer], srecv.at[:, row_at(slot, tok), :]),
            (kvsend.at[peer, 0], crecv.at[0, row_at(slot, crows), :]),
            (kvsend.at[peer, 1], crecv.at[1, row_at(slot, crows), :]),
            (fsend.at[peer], frecv.at[row_at(slot, held), :]),
            (osend.at[:, row_at(peer, tok), :], orecv.at[slot]),
        )[kind]
        return pltpu.make_async_remote_copy(
            src_ref=src,
            dst_ref=dst,
            send_sem=s_sem.at[kind, k],
            recv_sem=r_sem.at[kind, k],
            device_id={"seq": peer},
        )

    def arrive(kind):
        for k in range(1, S):
            exchange(kind, k, lax.rem(me + S - k, S)).wait_recv()

    pl.semaphore_wait(barrier, S - 1 + N - 1)
    for k in range(1, S):
        for kind in (0, 1, 2):
            exchange(kind, k, me).start()

    loads = []
    for e in range(local_experts):
        loads.append(pltpu.make_async_copy(gu_hbm.at[e], gu_v.at[e], load_sem.at[0, e]))
        loads.append(pltpu.make_async_copy(dn_hbm.at[e], dn_v.at[e], load_sem.at[1, e]))

    fresh = jnp.dot(held_ref[...], kw_ref[...], preferred_element_type=f32)
    low_part = lax.broadcasted_iota(jnp.int32, fresh.shape, 1) % HD < HD // 2
    partner = jnp.where(
        low_part,
        pltpu.roll(fresh, fresh.shape[1] - HD // 2, 1),
        pltpu.roll(fresh, HD // 2, 1),
    )
    fresh = fresh * jnp.tile(cos_ref[...], (1, KVH // 2)) + partner * jnp.tile(
        sin_ref[...], (1, KVH // 2)
    )
    for h in range(KVH):
        cols = slice((h // 2) * 2 * HD, (h // 2 + 1) * 2 * HD)
        odd = h % 2 == 1
        fsend[h] = join(fresh[:held, cols], odd, fresh[held:, cols], not odd)
    for k in range(1, S):
        exchange(4, k, me).start()
    for k in range(1, S):
        exchange(3, k, me).start()
    for load in loads:
        load.start()

    qrecv[:, row_at(me, tok), :] = qsend[me]
    srecv[:, row_at(me, tok), :] = stsend[me]
    crecv[:, row_at(me, crows), :] = kvsend[me]
    frecv[row_at(me, held), :] = fsend[me]

    expert_row = lax.broadcasted_iota(jnp.int32, (128, tok), 0)
    for r in range(2):
        dense = jnp.zeros((128, tok), f32)
        for k in range(TOP):
            hit = routes_ref[r, k : k + 1, :] == expert_row
            dense = dense + jnp.where(hit, rw_ref[r, k : k + 1, :], 0.0)
        wrecv[mz, r * tok : (r + 1) * tok, :] = dense.T

    def share_copy(k, slot):
        return pltpu.make_async_remote_copy(
            src_ref=wrecv.at[mz],
            dst_ref=wrecv.at[slot],
            send_sem=zs_sem.at[0, k],
            recv_sem=zr_sem.at[0, k],
            device_id={"req": lax.rem(mz + k, N)},
        )

    def back_copy(r, k, slot):
        peer = lax.rem(mz + k, N)
        return pltpu.make_async_remote_copy(
            src_ref=psend.at[r, peer],
            dst_ref=precv.at[r, slot],
            send_sem=zs_sem.at[1 + r, k],
            recv_sem=zr_sem.at[1 + r, k],
            device_id={"req": peer},
        )

    def token_copy(r, origin, way):
        return pltpu.make_async_remote_copy(
            src_ref=trecv.at[r, origin],
            dst_ref=trecv.at[r, origin],
            send_sem=ts_sem.at[way, r, origin],
            recv_sem=tr_sem.at[r, origin],
            device_id={"req": mz + 1 if way == 0 else mz - 1},
        )

    def send_tokens(r, origin, way):
        @pl.when(mz < N - 1 if way == 0 else mz > 0)
        def _():
            token_copy(r, origin, way).start()

    def relay(d, r):
        @pl.when(mz - d >= 0)
        def _():
            token_copy(r, mz - d, 0).wait_recv()
            send_tokens(r, mz - d, 0)

        @pl.when(mz + d < N)
        def _():
            token_copy(r, mz + d, 1).wait_recv()
            send_tokens(r, mz + d, 1)

    for k in range(1, N):
        share_copy(k, mz).start()

    for kind in (0, 1, 2, 4):
        arrive(kind)
    for r in range(2):
        if r == 1:
            arrive(3)
        key_half = (lanes(crows) < HD) if r == 0 else (lanes(crows) >= HD)
        ones = jnp.ones((S * held, 2 * HD), bf16)
        spread = jnp.concatenate([frecv[...], ones], axis=1)
        wanted = rec_ref[r : r + 1, :]

        def place(i, carry):
            rows = row_at(i, crows)
            kv = crecv[r, rows, :].astype(f32)
            where_to = lax.broadcasted_iota(jnp.int32, (crows, S * held), 0) + i * crows
            hit = jnp.where(where_to == wanted, 1.0, 0.0).astype(bf16)
            both = jnp.dot(hit, spread, preferred_element_type=f32)
            keys = jnp.where(both[:, 2 * HD :] > 0.5, both[:, : 2 * HD], kv)
            kbuf[rows, :] = jnp.where(key_half, keys, 0.0).astype(bf16)
            vbuf[rows, :] = jnp.where(key_half, 1.0, kv).astype(bf16)
            return carry

        lax.fori_loop(0, S, place, 0)
        step = srecv[r].astype(f32)
        step_half = (lanes(stotal) < HD) if r == 0 else (lanes(stotal) >= HD)
        kbuf[ctotal:, :] = jnp.where(step_half, step, 0.0).astype(bf16)
        vbuf[ctotal:, :] = jnp.where(step_half, 1.0, step).astype(bf16)
        position = lax.broadcasted_iota(jnp.int32, (1, ctotal), 1)
        open_row = (position >= spans_ref[r, 0]) & (position < spans_ref[r, 1])
        bias = jnp.where(open_row, 0.0, NEG)
        causal = lax.broadcasted_iota(jnp.int32, (stotal, stotal), 1) <= lax.broadcasted_iota(
            jnp.int32, (stotal, stotal), 0
        )
        contract = (((1,), (1,)), ((), ()))

        def attend(g, carry):
            query = qrecv[g]
            old = lax.dot_general(
                query, kbuf[:ctotal, :], contract, preferred_element_type=f32
            ) + bias
            new = lax.dot_general(query, kbuf[ctotal:, :], contract, preferred_element_type=f32)
            new = jnp.where(causal, new, NEG)
            highest = jnp.maximum(
                jnp.max(old, axis=-1, keepdims=True), jnp.max(new, axis=-1, keepdims=True)
            )
            mixed = jnp.dot(
                jnp.exp(old - highest).astype(bf16), vbuf[:ctotal, :], preferred_element_type=f32
            ) + jnp.dot(
                jnp.exp(new - highest).astype(bf16), vbuf[ctotal:, :], preferred_element_type=f32
            )
            mixed = mixed / pltpu.roll(mixed, HD, 1)
            if r == 0:
                osend[g] = mixed.astype(bf16)
            else:
                osend[g] = jnp.where(
                    lanes(stotal) < HD, mixed, osend[g].astype(f32)
                ).astype(bf16)
            return carry

        lax.fori_loop(0, groups, attend, 0)

    for k in range(1, S):
        exchange(5, k, me).start()
    orecv[me] = osend[:, row_at(me, tok), :]
    arrive(5)
    for pair in range(H // 2):
        first, second = 2 * pair, 2 * pair + 1
        one = orecv[first // groups, first % groups]
        two = orecv[second // groups, second % groups]
        cols = slice(pair * 2 * HD, (pair + 1) * 2 * HD)
        att[:tok, cols] = join(one, True, two, False)
        att[tok:, cols] = join(one, False, two, True)
    attended = att[...].astype(f32)
    mean_square = jnp.mean(attended * attended, axis=-1, keepdims=True)
    normed = (attended * lax.rsqrt(mean_square + 1e-06) * gain_ref[...].reshape(1, width)).astype(bf16)
    for r in range(2):
        trecv[r, mz] = normed[r * tok : (r + 1) * tok]
        for way in range(2):
            send_tokens(r, mz, way)
    for k in range(1, N):
        share_copy(k, lax.rem(mz + N - k, N)).wait_recv()
    for load in loads:
        load.wait()
    for d in range(1, N - 1):
        for r in range(2):
            relay(d, r)
    rows_total = N * tok
    for r in range(2):
        relay(N - 1, r)
        total[...] = jnp.zeros_like(total)

        def expert(e, carry):
            tokens = trecv[r].reshape(rows_total, width)
            hidden = jnp.dot(tokens, gu_v[e], preferred_element_type=f32)
            gate, up = hidden[:, :FF], hidden[:, FF:]
            active = (gate / (1.0 + jnp.exp(-gate)) * up).astype(bf16)
            result = jnp.dot(active, dn_v[e], preferred_element_type=f32).astype(bf16)
            weights = wrecv[:, r * tok : (r + 1) * tok, :].reshape(rows_total, 128)
            lane = lax.broadcasted_iota(jnp.int32, weights.shape, 1)
            share = jnp.sum(
                jnp.where(lane == mz * local_experts + e, weights, 0.0), axis=1, keepdims=True
            )
            total[...] += result.astype(f32) * share
            return carry

        lax.fori_loop(0, local_experts, expert, 0)
        psend[r] = total[...].astype(bf16).reshape(N, tok, width)
        for k in range(1, N):
            back_copy(r, k, mz).start()
    for r in range(2):
        rows = slice(r * tok, (r + 1) * tok)
        mixture = att[rows, :].astype(f32) + psend[r, mz].astype(f32)
        for k in range(1, N):
            back_copy(r, k, lax.rem(mz + N - k, N)).wait_recv()
        for k in range(1, N):
            mixture = mixture + precv[r, lax.rem(mz + N - k, N)].astype(f32)
        out_ref[rows, :] = mixture.astype(bf16)
    for kind in range(6):
        for k in range(1, S):
            exchange(kind, k, me).wait_send()
    for k in range(1, N):
        share_copy(k, mz).wait_send()
        for r in range(2):
            back_copy(r, k, mz).wait_send()
    for r in range(2):
        for origin in range(N):

            @pl.when((origin <= mz) & (mz < N - 1))
            def _():
                token_copy(r, origin, 0).wait_send()

            @pl.when((origin >= mz) & (mz > 0))
            def _():
                token_copy(r, origin, 1).wait_send()


def head_parallel_body(
    queries,
    new_kv,
    cache_kv,
    cache_spans,
    recompute_rows,
    held_states,
    key_weight,
    norm_gain,
    routes,
    route_weights,
    expert_gate_up,
    expert_down,
):
    seq_index = lax.axis_index("seq")
    S = lax.axis_size("seq")
    N = lax.axis_size("req")
    req_rows, tok, width = queries.shape
    crows = cache_kv.shape[2]
    held = held_states.shape[1]
    local_experts = expert_gate_up.shape[0]
    groups = H // KVH
    bf16, f32 = jnp.bfloat16, jnp.float32
    positions = lax.dynamic_slice_in_dim(recompute_rows, seq_index * held, held, 1)
    half = HD // 2
    inverse = THETA ** (-(jnp.arange(half).astype(f32) * (2.0 / HD)))
    angles = positions.reshape(req_rows * held, 1).astype(f32) * inverse
    cosine, sine = jnp.cos(angles), jnp.sin(angles)
    cos_table = jnp.concatenate([cosine] * 4, axis=1)
    sin_table = jnp.concatenate([-sine, sine, -sine, sine], axis=1)
    vmem = pl.BlockSpec(memory_space=pltpu.VMEM)
    smem = pl.BlockSpec(memory_space=pltpu.SMEM)
    hbm = pl.BlockSpec(memory_space=pl.ANY)
    lane = 2 * HD
    rows = req_rows * tok
    out = pl.pallas_call(
        layer_kernel,
        out_shape=jax.ShapeDtypeStruct((rows, width), bf16),
        in_specs=[smem] + [vmem] * 11 + [hbm, hbm],
        out_specs=vmem,
        scratch_shapes=[
            pltpu.VMEM(expert_gate_up.shape, bf16),
            pltpu.VMEM(expert_down.shape, bf16),
            pltpu.VMEM((S, 2, crows, lane), bf16),
            pltpu.VMEM((S, 2, tok, lane), bf16),
            pltpu.VMEM((S, groups, tok, lane), bf16),
            pltpu.VMEM((S, held, lane), bf16),
            pltpu.VMEM((groups, S * tok, lane), bf16),
            pltpu.VMEM((2, S * crows, lane), bf16),
            pltpu.VMEM((2, S * tok, lane), bf16),
            pltpu.VMEM((groups, S * tok, lane), bf16),
            pltpu.VMEM((S * held, lane), bf16),
            pltpu.VMEM((S, groups, tok, lane), bf16),
            pltpu.VMEM((S * (crows + tok), lane), bf16),
            pltpu.VMEM((S * (crows + tok), lane), bf16),
            pltpu.VMEM((rows, width), bf16),
            pltpu.VMEM((2, N, tok, width), bf16),
            pltpu.VMEM((N, rows, 128), f32),
            pltpu.VMEM((N * tok, width), f32),
            pltpu.VMEM((2, N, tok, width), bf16),
            pltpu.VMEM((2, N, tok, width), bf16),
            pltpu.SemaphoreType.DMA((2, local_experts)),
            pltpu.SemaphoreType.DMA((6, S)),
            pltpu.SemaphoreType.DMA((6, S)),
            pltpu.SemaphoreType.DMA((3, N)),
            pltpu.SemaphoreType.DMA((3, N)),
            pltpu.SemaphoreType.DMA((2, 2, N)),
            pltpu.SemaphoreType.DMA((2, N)),
        ],
        compiler_params=pltpu.CompilerParams(
            collective_id=0, has_side_effects=True, vmem_limit_bytes=60 << 20
        ),
        name="layer",
    )(
        cache_spans,
        recompute_rows,
        cos_table,
        sin_table,
        queries,
        new_kv,
        cache_kv,
        held_states.reshape(req_rows * held, width),
        key_weight,
        norm_gain,
        jnp.transpose(routes, (0, 2, 1)),
        jnp.transpose(route_weights, (0, 2, 1)),
        expert_gate_up,
        expert_down,
    )
    return out.reshape(req_rows, tok, width)


def solution(mesh):
    body = head_parallel_body if mesh.shape["seq"] == KVH else body_wide
    in_specs = (
        P("req", "seq", None),
        P(None, "req", "seq", None),
        P(None, "req", "seq", None),
        P("req", None),
        P("req", None),
        P("req", "seq", None),
        P(),
        P(),
        P("req", "seq", None),
        P("req", "seq", None),
        P("req", None, None),
        P("req", None, None),
    )
    out_specs = P("req", "seq", None)
    return jax.shard_map(body, mesh=mesh, in_specs=in_specs, out_specs=out_specs, check_vma=False)
```

```python
import jax
import jax.numpy as jnp
from jax import lax
from jax.experimental import pallas as pl
from jax.experimental.pallas import tpu as pltpu
from jax.sharding import PartitionSpec as P

H = 24
KVH = 8
HD = 64
FF = 512
TOP = 8
CAP = 16


NEG = -1e30
THETA = 10000.0


def rotate(key_heads, positions):
    half_dim = key_heads.shape[-1] // 2
    exponent = jnp.arange(half_dim).astype(jnp.float32) * (2.0 / key_heads.shape[-1])
    inverse = THETA ** (-exponent)
    angles = positions.astype(jnp.float32)[..., None] * inverse
    cosine = jnp.cos(angles)[..., None, :]
    sine_part = jnp.sin(angles)[..., None, :]
    lower_half = key_heads[..., :half_dim]
    upper_half = key_heads[..., half_dim:]
    return jnp.concatenate(
        [
            lower_half * cosine - upper_half * sine_part,
            upper_half * cosine + lower_half * sine_part,
        ],
        axis=-1,
    )


def partial_attend(packed):
    query_rows, key_rows, value_rows, allowed = packed
    query_count, model_width = query_rows.shape
    key_count = key_rows.shape[0]
    groups = H // KVH
    query_heads = query_rows.reshape(query_count, KVH, groups, HD)
    key_heads = key_rows.reshape(key_count, KVH, HD)
    value_heads = value_rows.reshape(key_count, KVH, HD)
    scores = jnp.einsum(
        "qkgd,nkd->kgqn", query_heads, key_heads, preferred_element_type=jnp.float32
    ) * HD ** (-0.5)
    scores = jnp.where(allowed[None, None, :, :], scores, NEG)
    highest = jnp.max(scores, axis=-1, keepdims=True)
    exps = jnp.exp(scores - highest)
    totals = jnp.sum(exps, axis=-1)
    weights = exps.astype(jnp.bfloat16)
    mixed_rows = jnp.einsum(
        "kgqn,nkd->qkgd", weights, value_heads, preferred_element_type=jnp.float32
    )
    mixed_rows = mixed_rows / jnp.transpose(totals, (2, 0, 1))[..., None]
    log_total = highest[..., 0] + jnp.log(totals)
    log_rows = jnp.transpose(log_total, (2, 0, 1)).reshape(query_count, H)
    return (mixed_rows.reshape(query_count, model_width), log_rows)


def body_wide(
    queries,
    new_kv,
    cache_kv,
    cache_spans,
    recompute_rows,
    held_states,
    key_weight,
    norm_gain,
    routes,
    route_weights,
    expert_gate_up,
    expert_down,
):
    seq_index = lax.axis_index("seq")
    seq_count = lax.axis_size("seq")
    owner_count = lax.axis_size("req")
    req_rows, tok_rows, model_width = queries.shape
    cache_rows = cache_kv.shape[2]
    held_rows = held_states.shape[1]
    local_experts = expert_gate_up.shape[0]
    expert_total = owner_count * local_experts
    my_positions = lax.dynamic_slice_in_dim(recompute_rows, seq_index * held_rows, held_rows, 1)
    projected = jnp.dot(
        held_states.reshape(req_rows * held_rows, model_width),
        key_weight,
        preferred_element_type=jnp.float32,
    )
    rotated = rotate(projected.reshape(req_rows, held_rows, KVH, HD), my_positions)
    rotated = rotated.reshape(req_rows, held_rows, KVH * HD).astype(jnp.bfloat16)
    fresh_rows = lax.all_gather(rotated, "seq", axis=1, tiled=True)
    cache_positions = seq_index * cache_rows + jnp.arange(cache_rows)
    hit_table = recompute_rows[:, None, :] == cache_positions[None, :, None]
    placed = jnp.einsum(
        "rcm,rmk->rck",
        hit_table.astype(jnp.bfloat16),
        fresh_rows,
        preferred_element_type=jnp.float32,
    ).astype(jnp.bfloat16)
    cache_keys = jnp.where(jnp.any(hit_table, axis=2)[:, :, None], placed, cache_kv[0])
    span_start = cache_spans[:, 0:1]
    span_end = cache_spans[:, 1:2]
    all_queries = lax.all_gather(queries, "seq", axis=1, tiled=True)
    step_total = all_queries.shape[1]
    cache_allowed = (cache_positions[None, :] >= span_start) & (cache_positions[None, :] < span_end)
    key_positions = seq_index * tok_rows + jnp.arange(tok_rows)
    step_allowed = key_positions[None, :] <= jnp.arange(step_total)[:, None]
    allowed = jnp.concatenate(
        [
            jnp.broadcast_to(cache_allowed[:, None, :], (req_rows, step_total, cache_rows)),
            jnp.broadcast_to(step_allowed[None], (req_rows, step_total, tok_rows)),
        ],
        axis=2,
    )
    key_rows = jnp.concatenate([cache_keys, new_kv[0]], axis=1)
    value_rows = jnp.concatenate([cache_kv[1], new_kv[1]], axis=1)
    part_out, part_log = lax.map(partial_attend, (all_queries, key_rows, value_rows, allowed))
    piece_out, piece_log = (
        lax.all_to_all(part_out[None], "seq", split_axis=2, concat_axis=0, tiled=True),
        lax.all_to_all(part_log[None], "seq", split_axis=2, concat_axis=0, tiled=True),
    )
    best_log = jnp.max(piece_log, axis=0)
    factors = jnp.exp(piece_log - best_log[None])
    factor_sum = jnp.sum(factors, axis=0)
    spread_out = piece_out.reshape(seq_count, req_rows, tok_rows, H, HD)
    combined = jnp.sum(spread_out * factors[..., None], axis=0) / factor_sum[..., None]
    attended_f = combined.reshape(req_rows, tok_rows, model_width)
    attended = attended_f.astype(jnp.bfloat16)
    attended_f = attended.astype(jnp.float32)
    mean_square = jnp.mean(attended_f * attended_f, axis=-1, keepdims=True)
    normed = (attended_f * lax.rsqrt(mean_square + 1e-06) * norm_gain).astype(jnp.bfloat16)
    route_flat = routes.reshape(req_rows, tok_rows * TOP)
    expert_match = (route_flat[:, :, None] == jnp.arange(expert_total)[None, None, :]).astype(
        jnp.int32
    )
    earlier = jnp.cumsum(expert_match, axis=1) - expert_match
    slot_index = jnp.sum(earlier * expert_match, axis=2)
    target = route_flat * CAP + slot_index
    slot_match = target[:, :, None] == jnp.arange(expert_total * CAP)[None, None, :]
    dispatch = jnp.any(
        slot_match.reshape(req_rows, tok_rows, TOP, expert_total * CAP), axis=2
    ).astype(jnp.bfloat16)
    dispatch = dispatch.reshape(req_rows, tok_rows, owner_count, local_experts, CAP)
    outgoing = jnp.einsum(
        "rtnec,rtd->nrecd", dispatch, normed, preferred_element_type=jnp.float32
    ).astype(jnp.bfloat16)
    hidden = jnp.einsum(
        "srecd,edf->srecf",
        lax.all_to_all(outgoing, "req", split_axis=0, concat_axis=0, tiled=True),
        expert_gate_up,
        preferred_element_type=jnp.float32,
    )
    active = (jax.nn.silu(hidden[..., :FF]) * hidden[..., FF:]).astype(jnp.bfloat16)
    result = jnp.einsum(
        "srecf,efd->srecd", active, expert_down, preferred_element_type=jnp.float32
    ).astype(jnp.bfloat16)
    returned = lax.all_to_all(result, "req", split_axis=0, concat_axis=0, tiled=True)
    owner_of = route_flat // local_experts
    local_of = route_flat % local_experts
    flat_index = (
        (owner_of * req_rows + jnp.arange(req_rows)[:, None]) * local_experts + local_of
    ) * CAP + slot_index
    returned_rows = jnp.take(returned.reshape(-1, model_width), flat_index.reshape(-1), axis=0)
    returned_rows = returned_rows.reshape(req_rows, tok_rows, TOP, model_width)
    mixture = jnp.einsum(
        "rtk,rtkd->rtd",
        route_weights,
        returned_rows.astype(jnp.float32),
        precision=lax.Precision.HIGHEST,
    )
    return (attended_f + mixture).astype(jnp.bfloat16)


def layer_kernel(
    spans_ref,
    rec_ref,
    cos_ref,
    sin_ref,
    q_ref,
    new_ref,
    cache_ref,
    held_ref,
    kw_ref,
    gain_ref,
    routes_ref,
    rw_ref,
    gu_hbm,
    dn_hbm,
    out_ref,
    gu_v,
    dn_v,
    kvsend,
    stsend,
    qsend,
    fsend,
    osend,
    crecv,
    srecv,
    qrecv,
    frecv,
    orecv,
    kbuf,
    vbuf,
    att,
    trecv,
    wrecv,
    total,
    psend,
    precv,
    load_sem,
    s_sem,
    r_sem,
    zs_sem,
    zr_sem,
    ts_sem,
    tr_sem,
):
    bf16 = jnp.bfloat16
    f32 = jnp.float32
    me = lax.axis_index("seq")
    S = lax.axis_size("seq")
    mz = lax.axis_index("req")
    N = lax.axis_size("req")
    groups = H // KVH
    tok = q_ref.shape[1]
    crows = cache_ref.shape[2]
    held = frecv.shape[0] // S
    width = q_ref.shape[2]
    local_experts = gu_v.shape[0]
    ctotal = S * crows
    stotal = S * tok

    barrier = pltpu.get_barrier_semaphore()
    for k in range(1, S):
        pl.semaphore_signal(barrier, inc=1, device_id={"seq": lax.rem(me + k, S)})
    for k in range(1, N):
        pl.semaphore_signal(barrier, inc=1, device_id={"req": lax.rem(mz + k, N)})

    def lanes(rows):
        return lax.broadcasted_iota(jnp.int32, (rows, 2 * HD), 1)

    def join(low, low_roll, high, high_roll, scale=None):
        a, b = low.astype(f32), high.astype(f32)
        a = pltpu.roll(a, HD, 1) if low_roll else a
        b = pltpu.roll(b, HD, 1) if high_roll else b
        c = jnp.where(lanes(a.shape[0]) < HD, a, b)
        return (c if scale is None else c * scale).astype(bf16)

    for h in range(KVH):
        cols = slice((h // 2) * 2 * HD, (h // 2 + 1) * 2 * HD)
        odd = h % 2 == 1
        for g in range(groups):
            c = h * groups + g
            qc = slice((c // 2) * 2 * HD, (c // 2 + 1) * 2 * HD)
            qsend[h, g] = join(q_ref[0, :, qc], c % 2 == 1, q_ref[1, :, qc], c % 2 == 0, HD**-0.5)
        for src, dst in ((cache_ref, kvsend), (new_ref, stsend)):
            dst[h, 0] = join(src[0, 0, :, cols], odd, src[1, 0, :, cols], not odd)
            dst[h, 1] = join(src[1, 1, :, cols], odd, src[0, 1, :, cols], not odd)

    def row_at(i, n):
        return pl.ds(pl.multiple_of(i * n, n), n)

    def exchange(kind, k, slot):
        peer = lax.rem(me + k, S)
        src, dst = (
            (qsend.at[peer], qrecv.at[:, row_at(slot, tok), :]),
            (stsend.at[peer], srecv.at[:, row_at(slot, tok), :]),
            (kvsend.at[peer, 0], crecv.at[0, row_at(slot, crows), :]),
            (kvsend.at[peer, 1], crecv.at[1, row_at(slot, crows), :]),
            (fsend.at[peer], frecv.at[row_at(slot, held), :]),
            (osend.at[:, row_at(peer, tok), :], orecv.at[slot]),
        )[kind]
        return pltpu.make_async_remote_copy(
            src_ref=src,
            dst_ref=dst,
            send_sem=s_sem.at[kind, k],
            recv_sem=r_sem.at[kind, k],
            device_id={"seq": peer},
        )

    def arrive(kind):
        for k in range(1, S):
            exchange(kind, k, lax.rem(me + S - k, S)).wait_recv()

    pl.semaphore_wait(barrier, S - 1 + N - 1)
    for k in range(1, S):
        for kind in (0, 1, 2):
            exchange(kind, k, me).start()

    loads = []
    for e in range(local_experts):
        loads.append(pltpu.make_async_copy(gu_hbm.at[e], gu_v.at[e], load_sem.at[0, e]))
        loads.append(pltpu.make_async_copy(dn_hbm.at[e], dn_v.at[e], load_sem.at[1, e]))

    fresh = jnp.dot(held_ref[...], kw_ref[...], preferred_element_type=f32)
    low_part = lax.broadcasted_iota(jnp.int32, fresh.shape, 1) % HD < HD // 2
    partner = jnp.where(
        low_part,
        pltpu.roll(fresh, fresh.shape[1] - HD // 2, 1),
        pltpu.roll(fresh, HD // 2, 1),
    )
    cosine, sine = cos_ref[...], sin_ref[...]
    cos_table = jnp.concatenate([cosine] * 4, axis=1)
    sin_table = jnp.concatenate([-sine, sine, -sine, sine], axis=1)
    fresh = fresh * jnp.tile(cos_table, (1, KVH // 2)) + partner * jnp.tile(
        sin_table, (1, KVH // 2)
    )
    for h in range(KVH):
        cols = slice((h // 2) * 2 * HD, (h // 2 + 1) * 2 * HD)
        odd = h % 2 == 1
        fsend[h] = join(fresh[:held, cols], odd, fresh[held:, cols], not odd)
    for k in range(1, S):
        exchange(4, k, me).start()
    for k in range(1, S):
        exchange(3, k, me).start()
    for load in loads:
        load.start()

    qrecv[:, row_at(me, tok), :] = qsend[me]
    srecv[:, row_at(me, tok), :] = stsend[me]
    crecv[:, row_at(me, crows), :] = kvsend[me]
    frecv[row_at(me, held), :] = fsend[me]

    expert_row = lax.broadcasted_iota(jnp.int32, (128, tok), 0)
    for r in range(2):
        dense = jnp.zeros((128, tok), f32)
        for k in range(TOP):
            hit = routes_ref[r, k : k + 1, :] == expert_row
            dense = dense + jnp.where(hit, rw_ref[r, k : k + 1, :], 0.0)
        wrecv[mz, r * tok : (r + 1) * tok, :] = dense.T

    def share_copy(k, slot):
        return pltpu.make_async_remote_copy(
            src_ref=wrecv.at[mz],
            dst_ref=wrecv.at[slot],
            send_sem=zs_sem.at[0, k],
            recv_sem=zr_sem.at[0, k],
            device_id={"req": lax.rem(mz + k, N)},
        )

    def back_copy(r, k, slot):
        peer = lax.rem(mz + k, N)
        return pltpu.make_async_remote_copy(
            src_ref=psend.at[r, peer],
            dst_ref=precv.at[r, slot],
            send_sem=zs_sem.at[1 + r, k],
            recv_sem=zr_sem.at[1 + r, k],
            device_id={"req": peer},
        )

    def token_copy(r, origin, way):
        return pltpu.make_async_remote_copy(
            src_ref=trecv.at[r, origin],
            dst_ref=trecv.at[r, origin],
            send_sem=ts_sem.at[way, r, origin],
            recv_sem=tr_sem.at[r, origin],
            device_id={"req": mz + 1 if way == 0 else mz - 1},
        )

    def send_tokens(r, origin, way):
        @pl.when(mz < N - 1 if way == 0 else mz > 0)
        def _():
            token_copy(r, origin, way).start()

    def relay(d, r):
        @pl.when(mz - d >= 0)
        def _():
            token_copy(r, mz - d, 0).wait_recv()
            send_tokens(r, mz - d, 0)

        @pl.when(mz + d < N)
        def _():
            token_copy(r, mz + d, 1).wait_recv()
            send_tokens(r, mz + d, 1)

    for k in range(1, N):
        share_copy(k, mz).start()

    for kind in (0, 1, 2, 4):
        arrive(kind)
    for r in range(2):
        if r == 1:
            arrive(3)
        key_half = (lanes(crows) < HD) if r == 0 else (lanes(crows) >= HD)
        ones = jnp.ones((S * held, 2 * HD), bf16)
        spread = jnp.concatenate([frecv[...], ones], axis=1)
        wanted = rec_ref[r : r + 1, :]

        def place(i, carry):
            rows = row_at(i, crows)
            kv = crecv[r, rows, :].astype(f32)
            where_to = lax.broadcasted_iota(jnp.int32, (crows, S * held), 0) + i * crows
            hit = jnp.where(where_to == wanted, 1.0, 0.0).astype(bf16)
            both = jnp.dot(hit, spread, preferred_element_type=f32)
            keys = jnp.where(both[:, 2 * HD :] > 0.5, both[:, : 2 * HD], kv)
            kbuf[rows, :] = jnp.where(key_half, keys, 0.0).astype(bf16)
            vbuf[rows, :] = jnp.where(key_half, 1.0, kv).astype(bf16)
            return carry

        lax.fori_loop(0, S, place, 0)
        step = srecv[r].astype(f32)
        step_half = (lanes(stotal) < HD) if r == 0 else (lanes(stotal) >= HD)
        kbuf[ctotal:, :] = jnp.where(step_half, step, 0.0).astype(bf16)
        vbuf[ctotal:, :] = jnp.where(step_half, 1.0, step).astype(bf16)
        position = lax.broadcasted_iota(jnp.int32, (1, ctotal), 1)
        open_row = (position >= spans_ref[r, 0]) & (position < spans_ref[r, 1])
        bias = jnp.where(open_row, 0.0, NEG)
        causal = lax.broadcasted_iota(jnp.int32, (stotal, stotal), 1) <= lax.broadcasted_iota(
            jnp.int32, (stotal, stotal), 0
        )
        contract = (((1,), (1,)), ((), ()))

        def attend(g, carry):
            query = qrecv[g]
            old = lax.dot_general(
                query, kbuf[:ctotal, :], contract, preferred_element_type=f32
            ) + bias
            new = lax.dot_general(query, kbuf[ctotal:, :], contract, preferred_element_type=f32)
            new = jnp.where(causal, new, NEG)
            highest = jnp.maximum(
                jnp.max(old, axis=-1, keepdims=True), jnp.max(new, axis=-1, keepdims=True)
            )
            mixed = jnp.dot(
                jnp.exp(old - highest).astype(bf16), vbuf[:ctotal, :], preferred_element_type=f32
            ) + jnp.dot(
                jnp.exp(new - highest).astype(bf16), vbuf[ctotal:, :], preferred_element_type=f32
            )
            mixed = mixed / pltpu.roll(mixed, HD, 1)
            if r == 0:
                osend[g] = mixed.astype(bf16)
            else:
                osend[g] = jnp.where(
                    lanes(stotal) < HD, mixed, osend[g].astype(f32)
                ).astype(bf16)
            return carry

        lax.fori_loop(0, groups, attend, 0)

    for k in range(1, S):
        exchange(5, k, me).start()
    orecv[me] = osend[:, row_at(me, tok), :]
    arrive(5)
    for pair in range(H // 2):
        first, second = 2 * pair, 2 * pair + 1
        one = orecv[first // groups, first % groups]
        two = orecv[second // groups, second % groups]
        cols = slice(pair * 2 * HD, (pair + 1) * 2 * HD)
        att[:tok, cols] = join(one, True, two, False)
        att[tok:, cols] = join(one, False, two, True)
    attended = att[...].astype(f32)
    mean_square = jnp.mean(attended * attended, axis=-1, keepdims=True)
    normed = (attended * lax.rsqrt(mean_square + 1e-06) * gain_ref[...].reshape(1, width)).astype(bf16)
    for r in range(2):
        trecv[r, mz] = normed[r * tok : (r + 1) * tok]
        for way in range(2):
            send_tokens(r, mz, way)
    for k in range(1, N):
        share_copy(k, lax.rem(mz + N - k, N)).wait_recv()
    for load in loads:
        load.wait()
    for d in range(1, N - 1):
        for r in range(2):
            relay(d, r)
    rows_total = N * tok
    for r in range(2):
        relay(N - 1, r)
        total[...] = jnp.zeros_like(total)

        def expert(e, carry):
            tokens = trecv[r].reshape(rows_total, width)
            hidden = jnp.dot(tokens, gu_v[e], preferred_element_type=f32)
            gate, up = hidden[:, :FF], hidden[:, FF:]
            active = (gate / (1.0 + jnp.exp(-gate)) * up).astype(bf16)
            result = jnp.dot(active, dn_v[e], preferred_element_type=f32).astype(bf16)
            weights = wrecv[:, r * tok : (r + 1) * tok, :].reshape(rows_total, 128)
            lane = lax.broadcasted_iota(jnp.int32, weights.shape, 1)
            share = jnp.sum(
                jnp.where(lane == mz * local_experts + e, weights, 0.0), axis=1, keepdims=True
            )
            total[...] += result.astype(f32) * share
            return carry

        lax.fori_loop(0, local_experts, expert, 0)
        psend[r] = total[...].astype(bf16).reshape(N, tok, width)
        for k in sorted(range(1, N), key=lambda k: abs(2 * k - N)):
            back_copy(r, k, mz).start()
    for r in range(2):
        rows = slice(r * tok, (r + 1) * tok)
        mixture = att[rows, :].astype(f32) + psend[r, mz].astype(f32)
        for k in range(1, N):
            back_copy(r, k, lax.rem(mz + N - k, N)).wait_recv()
        for k in range(1, N):
            mixture = mixture + precv[r, lax.rem(mz + N - k, N)].astype(f32)
        out_ref[rows, :] = mixture.astype(bf16)
    for kind in range(6):
        for k in range(1, S):
            exchange(kind, k, me).wait_send()
    for k in range(1, N):
        share_copy(k, mz).wait_send()
        for r in range(2):
            back_copy(r, k, mz).wait_send()
    for r in range(2):
        for origin in range(N):

            @pl.when((origin <= mz) & (mz < N - 1))
            def _():
                token_copy(r, origin, 0).wait_send()

            @pl.when((origin >= mz) & (mz > 0))
            def _():
                token_copy(r, origin, 1).wait_send()


def head_parallel_body(
    queries,
    new_kv,
    cache_kv,
    cache_spans,
    recompute_rows,
    held_states,
    key_weight,
    norm_gain,
    routes,
    route_weights,
    expert_gate_up,
    expert_down,
):
    seq_index = lax.axis_index("seq")
    S = lax.axis_size("seq")
    N = lax.axis_size("req")
    req_rows, tok, width = queries.shape
    crows = cache_kv.shape[2]
    held = held_states.shape[1]
    local_experts = expert_gate_up.shape[0]
    groups = H // KVH
    bf16, f32 = jnp.bfloat16, jnp.float32
    positions = lax.dynamic_slice_in_dim(recompute_rows, seq_index * held, held, 1)
    half = HD // 2
    inverse = THETA ** (-(jnp.arange(half).astype(f32) * (2.0 / HD)))
    angles = positions.reshape(req_rows * held, 1).astype(f32) * inverse
    cosine, sine = jnp.cos(angles), jnp.sin(angles)
    vmem = pl.BlockSpec(memory_space=pltpu.VMEM)
    smem = pl.BlockSpec(memory_space=pltpu.SMEM)
    hbm = pl.BlockSpec(memory_space=pl.ANY)
    lane = 2 * HD
    rows = req_rows * tok
    out = pl.pallas_call(
        layer_kernel,
        out_shape=jax.ShapeDtypeStruct((rows, width), bf16),
        in_specs=[smem] + [vmem] * 11 + [hbm, hbm],
        out_specs=vmem,
        scratch_shapes=[
            pltpu.VMEM(expert_gate_up.shape, bf16),
            pltpu.VMEM(expert_down.shape, bf16),
            pltpu.VMEM((S, 2, crows, lane), bf16),
            pltpu.VMEM((S, 2, tok, lane), bf16),
            pltpu.VMEM((S, groups, tok, lane), bf16),
            pltpu.VMEM((S, held, lane), bf16),
            pltpu.VMEM((groups, S * tok, lane), bf16),
            pltpu.VMEM((2, S * crows, lane), bf16),
            pltpu.VMEM((2, S * tok, lane), bf16),
            pltpu.VMEM((groups, S * tok, lane), bf16),
            pltpu.VMEM((S * held, lane), bf16),
            pltpu.VMEM((S, groups, tok, lane), bf16),
            pltpu.VMEM((S * (crows + tok), lane), bf16),
            pltpu.VMEM((S * (crows + tok), lane), bf16),
            pltpu.VMEM((rows, width), bf16),
            pltpu.VMEM((2, N, tok, width), bf16),
            pltpu.VMEM((N, rows, 128), f32),
            pltpu.VMEM((N * tok, width), f32),
            pltpu.VMEM((2, N, tok, width), bf16),
            pltpu.VMEM((2, N, tok, width), bf16),
            pltpu.SemaphoreType.DMA((2, local_experts)),
            pltpu.SemaphoreType.DMA((6, S)),
            pltpu.SemaphoreType.DMA((6, S)),
            pltpu.SemaphoreType.DMA((3, N)),
            pltpu.SemaphoreType.DMA((3, N)),
            pltpu.SemaphoreType.DMA((2, 2, N)),
            pltpu.SemaphoreType.DMA((2, N)),
        ],
        compiler_params=pltpu.CompilerParams(
            collective_id=0, has_side_effects=True, vmem_limit_bytes=60 << 20
        ),
        name="layer",
    )(
        cache_spans,
        recompute_rows,
        cosine,
        sine,
        queries,
        new_kv,
        cache_kv,
        held_states.reshape(req_rows * held, width),
        key_weight,
        norm_gain,
        jnp.transpose(routes, (0, 2, 1)),
        jnp.transpose(route_weights, (0, 2, 1)),
        expert_gate_up,
        expert_down,
    )
    return out.reshape(req_rows, tok, width)


def solution(mesh):
    body = head_parallel_body if mesh.shape["seq"] == KVH else body_wide
    in_specs = (
        P("req", "seq", None),
        P(None, "req", "seq", None),
        P(None, "req", "seq", None),
        P("req", None),
        P("req", None),
        P("req", "seq", None),
        P(),
        P(),
        P("req", "seq", None),
        P("req", "seq", None),
        P("req", None, None),
        P("req", None, None),
    )
    out_specs = P("req", "seq", None)
    return jax.shard_map(body, mesh=mesh, in_specs=in_specs, out_specs=out_specs, check_vma=False)
```
